256 devices in a mesh: real: 2 (over x_lo), bx: 16 (over y, x_hi, core), by: 8 (over z).
Axes of the slice: x: 4 (x_hi: 2, x_lo: 2; x = x_hi * 2 + x_lo), y: 4, z: 8, core: 2. Of those that a mesh axis runs over, the one named last changes fastest.
Arguments:
- current: float32 [2, 12, 3, 32, 64, 128], P('real', None, None, 'bx', 'by'), may hold values from -110 to 110
- previous: float32 [2, 12, 3, 32, 64, 128], P('real', None, None, 'bx', 'by'), may hold values from -110 to 110
- element_stiffness: float32 [24, 24], replicated, may hold values from -0.75 to 1.25, as said below
- preconditioner: float32 [2, 3, 32, 64, 128], P('real', None, 'bx', 'by'), may hold values from 0.04 to 0.16
- modulus: float32 [32, 64, 128], P('bx', 'by'), may hold values from 0.3 to 9.1
- density: float32 [32, 64, 128], P('bx', 'by'), may hold values from 0.5 to 2
- solid: int32 [2, 32, 64, 128], P('real', 'bx', 'by'), may hold values from 0 to 1, as said below
- clamped: int32 [32, 64], P('bx', 'by'), may hold values 0 or 1
Outputs:
- gram_stiff: float32 [2, 36, 36], P('real')
- gram_mass: float32 [2, 36, 36], P('real')
- search_block: float32 [2, 12, 3, 32, 64, 128], P('real', None, None, 'bx', 'by')
- sensitivity: float32 [32, 64, 128], P('bx', 'by', 'real')
The draws below stay inside these ranges and needn't reach their ends.
Inputs may be any that keep to these rules, and one draw needn't show every extreme that they name: `element_stiffness`: symmetric positive definite: the stiffness of a trilinear brick of unit edge for unit modulus and a Poisson ratio between 0.25 and 0.35, divided by its diagonal entry, plus a small positive definite part. 1 marks a solid element of that realization; a realization's solid elements include those of every realization before it. `clamped`: 1 marks a bottom-face node held in all three directions.
All inputs are finite; a program needn't handle non-finite values. No bound on the sum of `clamped` on one device may be relied on, other than what follows from the above.
Results may differ from the reference program's by a relative error of at most 0.00013.
Values sent between devices are 32-bit elements; how exact they have to be, the bound alone decides.
A program may use at most 64 MiB of HBM per device.

```python
import math
import jax
import jax.numpy as jnp
import numpy as np
from jax import lax

NZ = 128
COLS = 12
REALS = 2
GX = 32
GY = 64


def mixed_block(key, salt_code):
    key_base = jax.random.fold_in(key, salt_code)
    key_noise, key_mix = jax.random.split(key_base, 2)
    block_shape = (REALS, COLS, 3, GX, GY, NZ)
    noise_field = jnp.clip(jax.random.normal(key_noise, block_shape, jnp.float32), -4.0, 4.0)
    mixing = jnp.eye(COLS, dtype=jnp.float32) + jnp.clip(0.12 * jax.random.normal(key_mix, (COLS, COLS), jnp.float32), -0.5, 0.5)
    return jnp.einsum('rkdxyz,kj->rjdxyz', noise_field, mixing)


def draw_current(key, part):
    return mixed_block(key, 101)


def draw_previous(key, part):
    current_part = mixed_block(key, 101)
    fresh_part = mixed_block(key, 202)
    key_turn = jax.random.fold_in(key, 303)
    turning = jnp.eye(COLS, dtype=jnp.float32) + jnp.clip(0.1 * jax.random.normal(key_turn, (COLS, COLS), jnp.float32), -0.3, 0.3)
    blended = 0.6 * jnp.einsum('rkdxyz,kj->rjdxyz', current_part, turning) + 0.8 * fresh_part
    return jnp.clip(blended, -110.0, 110.0)


def brick_tables():
    offset = 0.5 / math.sqrt(3.0)
    places = [0.5 - offset, 0.5 + offset]
    tables = np.zeros((8, 6, 24), np.float32)
    point_index = 0
    for place_x in places:
        for place_y in places:
            for place_z in places:
                for corner_x in (0, 1):
                    for corner_y in (0, 1):
                        for corner_z in (0, 1):
                            column = 3 * (4 * corner_x + 2 * corner_y + corner_z)
                            value_x = place_x if corner_x else 1.0 - place_x
                            value_y = place_y if corner_y else 1.0 - place_y
                            value_z = place_z if corner_z else 1.0 - place_z
                            slope_x = 1.0 if corner_x else -1.0
                            slope_y = 1.0 if corner_y else -1.0
                            slope_z = 1.0 if corner_z else -1.0
                            grad_x = slope_x * value_y * value_z
                            grad_y = value_x * slope_y * value_z
                            grad_z = value_x * value_y * slope_z
                            tables[point_index, 0, column] = grad_x
                            tables[point_index, 1, column + 1] = grad_y
                            tables[point_index, 2, column + 2] = grad_z
                            tables[point_index, 3, column] = grad_y
                            tables[point_index, 3, column + 1] = grad_x
                            tables[point_index, 4, column + 1] = grad_z
                            tables[point_index, 4, column + 2] = grad_y
                            tables[point_index, 5, column + 2] = grad_x
                            tables[point_index, 5, column] = grad_z
                point_index += 1
    return tables


def draw_element_stiffness(key, part):
    key_ratio, key_extra = jax.random.split(jax.random.fold_in(key, 7))
    poisson_ratio = jax.random.uniform(key_ratio, (), jnp.float32, 0.25, 0.35)
    lame_first = poisson_ratio / ((1.0 + poisson_ratio) * (1.0 - 2.0 * poisson_ratio))
    shear_modulus = 0.5 / (1.0 + poisson_ratio)
    identity_three = jnp.eye(3, dtype=jnp.float32)
    zeros_three = jnp.zeros((3, 3), jnp.float32)
    upper_block = jnp.ones((3, 3), jnp.float32) * lame_first + 2.0 * shear_modulus * identity_three
    material = jnp.concatenate([jnp.concatenate([upper_block, zeros_three], 1), jnp.concatenate([zeros_three, shear_modulus * identity_three], 1)], 0)
    tables = jnp.asarray(brick_tables())
    brick_matrix = jnp.einsum('gsi,st,gtj->ij', tables, material, tables, precision=lax.Precision.HIGHEST) / 8.0
    brick_matrix = 0.5 * (brick_matrix + brick_matrix.T)
    brick_matrix = brick_matrix / brick_matrix[0, 0]
    extra_part = jnp.clip(jax.random.normal(key_extra, (24, 24), jnp.float32), -2.0, 2.0)
    positive_part = jnp.dot(extra_part, extra_part.T, precision=lax.Precision.HIGHEST)
    positive_part = 0.5 * (positive_part + positive_part.T)
    return brick_matrix + 0.05 * jnp.eye(24, dtype=jnp.float32) + 0.002 * positive_part


def draw_modulus(key, part):
    key_rough = jax.random.fold_in(key, 11)
    ramp_x = jnp.exp(jnp.log(3.0) * (jnp.arange(GX, dtype=jnp.float32) + 0.5) / GX)[:, None, None]
    reach_log = 0.7
    rough_part = jnp.exp(jax.random.uniform(key_rough, (GX, GY, NZ), jnp.float32, -reach_log, reach_log))
    return rough_part * ramp_x


def draw_solid(key, part):
    key_levels = jax.random.fold_in(key, 13)
    levels = jax.random.randint(key_levels, (GX, GY, NZ), 0, 100)
    cutoff = 45 + 40 * jnp.arange(REALS, dtype=jnp.int32) // max(REALS - 1, 1)
    return (levels[None] < cutoff[:, None, None, None]).astype(jnp.int32)


def plant(drawn, own_key, least, high):
    dims = drawn.shape
    spot = [jax.random.randint(jax.random.fold_in(own_key, axis), (), 0, dims[axis]) for axis in range(len(dims))]
    drawn = drawn.at[tuple(spot)].set(least)
    longest = dims.index(max(dims))
    spot[longest] = (spot[longest] + 1) % dims[longest]
    return drawn.at[tuple(spot)].set(high)


def shard_levels(rng, extent, cuts, low, largest):
    def one(axis_at, parts):
        steps = jax.random.uniform(jax.random.fold_in(jax.random.fold_in(rng, 6), axis_at), (parts,), jnp.float32, low / len(cuts), largest / len(cuts))
        return jnp.repeat(jnp.exp(steps), extent[axis_at] // parts).reshape((-1,) + (1,) * (len(extent) - axis_at - 1))

    gain = one(*cuts[0])
    for cut in cuts[1:]:
        gain = gain * one(*cut)
    return gain


def setup_inputs(seed: int = 0) -> dict:
    seeds = jax.random.split(jax.random.key(seed), 9)
    current = draw_current(jax.random.fold_in(seeds[8], 71), 0)
    previous = draw_previous(jax.random.fold_in(seeds[8], 71), 0)
    element_stiffness = draw_element_stiffness(jax.random.fold_in(seeds[8], 71), 0)
    preconditioner = jnp.clip(jnp.exp(math.log(0.16) - 1.3862944 * jax.random.uniform(seeds[3], (REALS, 3, GX, GY, NZ), jnp.float32) ** shard_levels(seeds[3], (REALS, 3, GX, GY, NZ), ((0, 2), (2, 16), (3, 8)), -0.2, 0.2)), 0.04, 0.16)
    modulus = draw_modulus(jax.random.fold_in(seeds[8], 71), 0)
    density = jnp.clip(jnp.exp(math.log(2.0) - 1.3862944 * jax.random.uniform(seeds[5], (GX, GY, NZ), jnp.float32) ** shard_levels(seeds[5], (GX, GY, NZ), ((0, 16), (1, 8)), -0.2, 0.2)), 0.5, 2.0)
    solid = draw_solid(jax.random.fold_in(seeds[8], 71), 0)
    clamped = plant((jax.random.randint(seeds[7], (GX, GY), 0, 4) < 1).astype(jnp.int32), jax.random.fold_in(seeds[7], 1), 0, 1)
    return dict(current=current, previous=previous, element_stiffness=element_stiffness, preconditioner=preconditioner, modulus=modulus, density=density, solid=solid, clamped=clamped)


highest = lax.Precision.HIGHEST
soft_power = 4.0
corner_list = [(0, 0, 0), (0, 0, 1), (0, 1, 0), (0, 1, 1), (1, 0, 0), (1, 0, 1), (1, 1, 0), (1, 1, 1)]


def corner_values(extended, size_x, size_y, size_z):
    return jnp.stack([extended[..., shift_x:shift_x + size_x, shift_y:shift_y + size_y, shift_z:shift_z + size_z] for shift_x, shift_y, shift_z in corner_list], 0)


def scatter_corners(pieces):
    leading = pieces.ndim - 4
    overall = 0.0
    for corner, (shift_x, shift_y, shift_z) in enumerate(corner_list):
        widths = [(0, 0)] * leading + [(shift_x, 1 - shift_x), (shift_y, 1 - shift_y), (shift_z, 1 - shift_z)]
        overall = overall + jnp.pad(pieces[corner], widths)
    return overall


def element_pass(extended, stiff_field, element_four):
    size_x, size_y, size_z = stiff_field.shape
    corner_vals = corner_values(extended, size_x, size_y, size_z)
    forces = jnp.einsum('adbe,bkexyz->akdxyz', element_four, corner_vals, precision=highest)
    energy_stiff = jnp.einsum('akdxyz,akdxyz->kxyz', corner_vals, forces, precision=highest)
    energy_mass = jnp.sum(corner_vals * corner_vals, axis=(0, 2)) * 0.125
    return scatter_corners(forces * stiff_field), energy_stiff, energy_mass


def stiffness_apply(block, stiff_field, free_mask, element_four):
    size_x, size_y, size_z = stiff_field.shape
    padded = jnp.pad(block, ((0, 0), (0, 0), (0, 1), (0, 1), (0, 1)))

    def single_column(column):
        assembled, energy_stiff, energy_mass = element_pass(column[None], stiff_field, element_four)
        return assembled[0], energy_stiff[0], energy_mass[0]

    assembled, energy_stiff, energy_mass = lax.map(single_column, padded)
    return assembled[:, :, :size_x, :size_y, :size_z] * free_mask, energy_stiff, energy_mass


def gram_matrix(left_blocks, right_blocks):
    gram_rows = []
    for left_block in left_blocks:
        flat_left = left_block.reshape(left_block.shape[0], -1)
        gram_rows.append(jnp.concatenate([jnp.einsum('ik,jk->ij', flat_left, right_block.reshape(right_block.shape[0], -1), precision=highest) for right_block in right_blocks], 1))
    return jnp.concatenate(gram_rows, 0)


def reference(current, previous, element_stiffness, preconditioner, modulus, density, solid, clamped):
    element_four = element_stiffness.reshape(8, 3, 8, 3)
    size_x, size_y, size_z = modulus.shape
    dof_count = 3.0 * size_x * size_y * size_z
    bottom = (jnp.arange(size_z) == 0).astype(jnp.float32)
    free_mask = 1.0 - clamped.astype(jnp.float32)[:, :, None] * bottom
    grams_stiff = []
    grams_mass = []
    searches = []
    records = []
    for realization in range(REALS):
        solid_share = solid[realization].astype(jnp.float32)
        stiff_field = modulus * (0.02 + 0.98 * solid_share)
        mass_field = density * (0.1 + 0.9 * solid_share)
        lumped = scatter_corners(jnp.stack([mass_field * 0.125] * 8, 0))[:size_x, :size_y, :size_z] * free_mask
        current_free = current[realization] * free_mask
        previous_free = previous[realization] * free_mask
        stiff_cur, energy_stiff, energy_mass = stiffness_apply(current_free, stiff_field, free_mask, element_four)
        stiff_prev, _, _ = stiffness_apply(previous_free, stiff_field, free_mask, element_four)
        mass_cur = lumped * current_free
        mass_prev = lumped * previous_free
        numerator = jnp.sum(current_free * stiff_cur, axis=(1, 2, 3, 4)) / dof_count
        denominator = jnp.sum(current_free * mass_cur, axis=(1, 2, 3, 4)) / dof_count
        quotient = numerator / denominator
        search = preconditioner[realization][None] * (stiff_cur - mass_cur * quotient[:, None, None, None, None])
        stiff_search, _, _ = stiffness_apply(search, stiff_field, free_mask, element_four)
        mass_search = lumped * search
        search_basis = [current_free, search, previous_free]
        grams_stiff.append(gram_matrix(search_basis, [stiff_cur, stiff_search, stiff_prev]) / dof_count)
        grams_mass.append(gram_matrix(search_basis, [mass_cur, mass_search, mass_prev]) / dof_count)
        searches.append(search)
        records.append((quotient, denominator, energy_stiff, energy_mass, stiff_field, mass_field))
    powered = [record[0] ** (-soft_power) for record in records]
    overall = jnp.sum(jnp.stack([jnp.sum(entry) for entry in powered]))
    sensitivity = jnp.zeros((size_x, size_y, size_z), jnp.float32)
    for entry, (quotient, denominator, energy_stiff, energy_mass, stiff_field, mass_field) in zip(powered, records):
        coefficient = entry / overall / denominator
        sensitivity = sensitivity + 3.0 * stiff_field * jnp.einsum('j,jxyz->xyz', coefficient, energy_stiff, precision=highest) - mass_field * jnp.einsum('j,jxyz->xyz', coefficient * quotient, energy_mass, precision=highest)
    return jnp.stack(grams_stiff), jnp.stack(grams_mass), jnp.stack(searches), sensitivity
```

```python
import functools

import jax
import jax.numpy as jnp
import numpy as np
from jax import lax
from jax.experimental import pallas as pl
from jax.experimental.pallas import tpu as pltpu
from jax.sharding import PartitionSpec as P

MESH = pl.DeviceIdType.MESH
F32 = jnp.float32
BF16 = jnp.bfloat16
COLS = 12
WIDE = 4 * COLS
PAIRS = COLS // 2
DIRS = [
    (1, 0, (0, 2), (0, 8), 3, 0),
    (-1, 0, (1, 1), (0, 8), 0, 0),
    (0, 1, (0, 2), (0, 2), 1, 8),
    (0, -1, (0, 2), (7, 1), 1, 10),
    (1, 1, (0, 2), (0, 2), 3, 8),
    (1, -1, (0, 2), (7, 1), 3, 10),
    (-1, 1, (1, 1), (0, 2), 0, 8),
    (-1, -1, (1, 1), (7, 1), 0, 10),
]
PREV_DIRS = [
    (1, 0, (0, 1), (0, 8), 2, 0),
    (0, 1, (0, 2), (0, 1), 0, 8),
    (1, 1, (0, 1), (0, 1), 2, 8),
]


def operator_tables():
    pick_row = np.zeros((256, 24), np.float32)
    pick_col = np.zeros((24, 384), np.float32)
    allow = np.zeros((2, 256, 192), np.float32)
    row_y = np.full(256, 99)
    row_b = np.zeros(256, int)
    for a in range(2):
        for b in range(2):
            for q in range(2):
                for d in range(3):
                    i = 3 * (4 * a + 2 * b + q) + d
                    for y in range(8):
                        m = a * 128 + ((b * 2 + q) * 3 + d) * 8 + y
                        pick_row[m, i], row_y[m], row_b[m] = 1, y, b
                    m = a * 128 + 96 + (b * 2 + q) * 8 + d
                    pick_row[m, i], row_y[m], row_b[m] = 1, 8, b
    for a in range(2):
        for d in range(3):
            for q in range(2):
                for row in range(11):
                    k = a * 96 + (d * 2 + q) * 16 + row
                    y = -1 if row == 10 else row
                    for b in range(2):
                        pick_col[3 * (4 * a + 2 * b + q) + d, b * 192 + k] = 1
                        allow[b, :, k] = (y - row_y + row_b == b).astype(np.float32)
    return pick_row, pick_col, allow


def pair_dot(left, right):
    return lax.dot_general(left, right, (((1,), (0,)), ((), ())), preferred_element_type=F32)


def exact_dot(left, right):
    return lax.dot_general(
        left,
        right,
        (((1,), (0,)), ((), ())),
        preferred_element_type=F32,
        precision=lax.Precision.HIGHEST,
    )


def halves(value):
    high = value.astype(BF16)
    return high, (value - high.astype(F32)).astype(BF16)


def lane_of(value):
    return lax.broadcasted_iota(jnp.int32, value.shape, 1)


def row_of(value):
    return lax.broadcasted_iota(jnp.int32, value.shape, 0)


def from_next_z(value):
    return jnp.where(lane_of(value) == 127, 0.0, pltpu.roll(value, 127, 1))


def to_next_z(value):
    return jnp.where(lane_of(value) == 0, 0.0, pltpu.roll(value, 1, 1))


def spread(row):
    return jnp.broadcast_to(row, (8, 128))


def from_lower_y(main, below):
    return jnp.where(row_of(main) == 0, spread(below), pltpu.roll(main, 1, 0))


def from_upper_y(main, above):
    return jnp.where(row_of(main) == 7, spread(above), pltpu.roll(main, 7, 0))


def stacked_rows(rows):
    out = jnp.zeros((8, 128), F32)
    at = row_of(out)
    for d, row in enumerate(rows):
        out = jnp.where(at == d, spread(row), out)
    return out


def halo_copies(sizes, refs, sems):
    bx, by = lax.axis_index("bx"), lax.axis_index("by")
    nx, ny = sizes
    send_sem, recv_sem = sems
    out = []
    jobs = [(DIRS, refs["fld"], refs["FE"]), (DIRS, refs["cur"], refs["XC"])]
    jobs.append((PREV_DIRS, refs["prev"], refs["XP"]))
    for dirs, source, target in jobs:
        for dx, dy, (x0, xn), (y0, yn), tx, ty in dirs:
            to_x, to_y = bx - dx, by - dy
            sends = (to_x >= 0) & (to_x < nx) & (to_y >= 0) & (to_y < ny)
            gets = (bx + dx >= 0) & (bx + dx < nx) & (by + dy >= 0) & (by + dy < ny)
            at = len(out)
            copy = pltpu.make_async_remote_copy(
                src_ref=source.at[:, :, x0 : x0 + xn, y0 : y0 + yn, :],
                dst_ref=target.at[:, :, tx : tx + xn, ty : ty + yn, :],
                send_sem=send_sem.at[at],
                recv_sem=recv_sem.at[at],
                device_id={"bx": to_x, "by": to_y},
                device_id_type=MESH,
            )
            out.append((copy, sends, gets))
    return out


N_HALO = 2 * len(DIRS) + len(PREV_DIRS)


def greet_neighbours(sizes, barrier):
    bx, by = lax.axis_index("bx"), lax.axis_index("by")
    nx, ny = sizes
    count = 0
    for dx in (-1, 0, 1):
        for dy in (-1, 0, 1):
            if dx == 0 and dy == 0:
                continue
            there = (bx + dx >= 0) & (bx + dx < nx) & (by + dy >= 0) & (by + dy < ny)

            @pl.when(there)
            def _():
                pl.semaphore_signal(
                    barrier,
                    inc=1,
                    device_id={"bx": bx + dx, "by": by + dy},
                    device_id_type=MESH,
                )

            count = count + there.astype(jnp.int32)
    return count


def local_copies(refs, sem):
    return [
        pltpu.make_async_copy(refs["fld"], refs["FE"].at[:, :, 1:3, 0:8, :], sem.at[0]),
        pltpu.make_async_copy(refs["cur"], refs["XC"].at[:, :, 1:3, 0:8, :], sem.at[1]),
        pltpu.make_async_copy(refs["prev"], refs["XP"].at[:, :, 0:2, 0:8, :], sem.at[2]),
    ]


def build_operator(refs):
    spread_rows = exact_dot(refs["pick_row"][...], refs["elem"][...])
    both = exact_dot(spread_rows, refs["pick_col"][...])
    full = refs["allow"][0] * both[:, 0:192] + refs["allow"][1] * both[:, 192:384]
    high, low = halves(full)
    for a in range(2):
        refs["WH"][a] = high[a * 128 : a * 128 + 128]
        refs["WL"][a] = low[a * 128 : a * 128 + 128]


def halo_kernel(sizes, names, *args):
    refs = dict(zip(names, args))
    for name in ("XC", "XP", "FE"):
        ref = refs[name]
        for i in range(ref.shape[0]):
            ref[i] = jnp.zeros(ref.shape[1:], F32)
    barrier = pltpu.get_barrier_semaphore()
    count = greet_neighbours(sizes, barrier)
    locals_ = local_copies(refs, refs["local_sem"])
    for copy in locals_:
        copy.start()
    pl.semaphore_wait(barrier, count)
    copies = halo_copies(sizes, refs, (refs["send_sem"], refs["recv_sem"]))
    for copy, sends, _ in copies:
        pl.when(sends)(copy.start)
    build_operator(refs)
    for copy in locals_:
        copy.wait()
    for copy, sends, gets in copies:
        pl.when(gets)(copy.wait_recv)
    for copy, sends, gets in copies:
        pl.when(sends)(copy.wait_send)


def prepare_fields(refs):
    FE, SS, LM, PM, P8 = refs["FE"], refs["SS"], refs["LM"], refs["PM"], refs["P8"]
    mass_sum = []
    for e in range(4):
        for kind in range(2):
            main, row8 = FE[0, kind, e, 0:8], FE[0, kind, e, 8:9]
            below = FE[0, kind, e, 10:11]
            lower = from_lower_y(main, below)
            here8, lower8 = spread(row8), spread(main[7:8])
            if kind == 0:
                SS[e, 0], SS[e, 1], SS[e, 2], SS[e, 3] = main, lower, here8, lower8
            else:
                mass_sum.append((main + lower, here8 + lower8))
    for n in range(3):
        for part in range(2):
            total = mass_sum[n][part] + mass_sum[n + 1][part]
            keep = FE[0, 2, n + 1, 0:8] if part == 0 else spread(FE[0, 2, n + 1, 8:9])
            LM[n, part] = (total + to_next_z(total)) * 0.125 * keep
        for d in range(3):
            PM[n, d] = FE[1, d, n + 1, 0:8] * FE[0, 2, n + 1, 0:8]
        P8[n] = stacked_rows([FE[1, d, n + 1, 8:9] * FE[0, 2, n + 1, 8:9] for d in range(3)])


def store_operand(high_ref, low_ref, lead, d, h, value):
    for q, plane in enumerate((value, from_next_z(value))):
        high, low = halves(plane)
        at = (*lead, slice((d * 2 + q) * 16, (d * 2 + q) * 16 + 16), slice(h * 128, h * 128 + 128))
        high_ref[at] = high
        low_ref[at] = low


def forces(refs, a, high, low):
    return (
        pair_dot(refs["WH"][a], high)
        + pair_dot(refs["WH"][a], low)
        + pair_dot(refs["WL"][a], high)
    )


def block_of(force, b, q, d, h):
    g = ((b * 2 + q) * 3 + d) * 8
    return force[g : g + 8, h * 128 : h * 128 + 128]


def block8_of(force, b, q, h):
    g = 96 + (b * 2 + q) * 8
    return force[g : g + 8, h * 128 : h * 128 + 128]


def add_to(store, key, value):
    store[key] = value if key not in store else store[key] + value


def current_pair(refs, p):
    XC, FE, VV, UH, UL = refs["XC"], refs["FE"], refs["VV"], refs["UH"], refs["UL"]
    SS, LM, PM, P8 = refs["SS"], refs["LM"], refs["PM"], refs["P8"]
    XS, KS, X8, K8 = refs["XS"], refs["KS"], refs["X8"], refs["K8"]
    for h in range(2):
        for x in range(5):
            keep = FE[0, 2, x]
            for d in range(3):
                value = XC[2 * p + h, d, x] * keep
                store_operand(UH, UL, (x,), d, h, value)
                VV[h, d, 0, x] = value
                VV[h, d, 1, x] = from_next_z(value)
    edge = {}
    for h in range(2):
        for q in range(2):
            for x in range(1, 4):
                edge[h, q, x] = stacked_rows([VV[h, d, q, x, 8:9] for d in range(3)])
    total, total8, energy, energy8 = {}, {}, {}, {}
    for e in range(4):
        high = UH[e : e + 2].reshape(192, 256)
        low = UL[e : e + 2].reshape(192, 256)
        for a in range(2):
            n = e - 1 + a
            if not 0 <= n <= 2:
                continue
            force = forces(refs, a, high, low)
            for h in range(2):
                for b in range(2):
                    for q in range(2):
                        for d in range(3):
                            block = block_of(force, b, q, d, h)
                            add_to(total, (n, d, q, h), SS[e, b] * block)
                            if e in (1, 2):
                                add_to(energy, (e, b, h), VV[h, d, q, e + a, 0:8] * block)
                        block = block8_of(force, b, q, h)
                        add_to(total8, (n, q, h), SS[e, 2 + b] * block)
                        if e in (1, 2) and b == 1:
                            add_to(energy8, (e, h), edge[h, q, e + a] * block)
    zero = jnp.zeros((8, 128), F32)
    for h in range(2):
        c = 2 * p + h
        for n in range(3):
            stiff8 = total8[n, 0, h] + to_next_z(total8[n, 1, h])
            first8 = P8[n] * stiff8
            second8 = P8[n] * LM[n, 1] * edge[h, 0, n + 1]
            for ref, col, value in (
                (X8, 0, edge[h, 0, n + 1]),
                (X8, 1, first8),
                (X8, 2, second8),
                (K8, 0, zero),
            ):
                ref[n, pl.ds(pl.multiple_of((col * COLS + c) * 8, 8), 8), :] = value
            for d in range(3):
                stiff = total[n, d, 0, h] + to_next_z(total[n, d, 1, h])
                here = VV[h, d, 0, n + 1, 0:8]
                first = PM[n, d] * stiff
                second = PM[n, d] * LM[n, 0] * here
                for ref, col, value in (
                    (XS, 0, here),
                    (XS, 1, first),
                    (XS, 2, second),
                    (KS, 0, stiff if n < 2 else zero),
                ):
                    at = pl.ds(pl.multiple_of((col * COLS + c) * 8, 8), 8)
                    ref[d * 3 + n, at, :] = value
                if n < 2:
                    refs["first"][c, d, n] = first
                    refs["second"][c, d, n] = second
                for kind, main, row8 in ((0, first, first8), (1, second, second8)):
                    plane = jnp.concatenate([main, spread(row8[d : d + 1])], 0)
                    store_operand(refs["U2H"], refs["U2L"], (kind * PAIRS + p, n), d, h, plane)
        for e in (1, 2):
            above = jnp.sum(energy8[e, h], axis=0, keepdims=True)
            refs["ES"][c, e - 1] = energy[e, 0, h] + from_upper_y(energy[e, 1, h], above)
            square = 0.0
            for x in (e, e + 1):
                for d in range(3):
                    for q in range(2):
                        square = square + VV[h, d, q, x] * VV[h, d, q, x]
            main = square[0:8]
            refs["EM"][c, e - 1] = (main + from_upper_y(main, square[8:9])) * 0.125


def previous_pair(refs, p):
    for h in range(2):
        c = 2 * p + h
        at = pl.ds(pl.multiple_of((3 * COLS + c) * 8, 8), 8)
        for n in range(3):
            rows = []
            for d in range(3):
                value = refs["XP"][c, d, n] * refs["FE"][0, 2, n + 1]
                store_operand(refs["U2H"], refs["U2L"], (2 * PAIRS + p, n), d, h, value)
                refs["XS"][d * 3 + n, at, :] = value[0:8]
                rows.append(value[8:9])
            refs["X8"][n, at, :] = stacked_rows(rows)


def second_pair(refs, p):
    SS, KS, K8 = refs["SS"], refs["KS"], refs["K8"]
    total, total8 = {}, {}
    for e in range(2):
        high = refs["U2H"][p, e : e + 2].reshape(192, 256)
        low = refs["U2L"][p, e : e + 2].reshape(192, 256)
        scale = [SS[e + 1, 0], jnp.where(row_of(SS[e + 1, 1]) == 0, 0.0, SS[e + 1, 1])]
        for a in range(2):
            n = e + a
            force = forces(refs, a, high, low)
            for h in range(2):
                for q in range(2):
                    for b in range(2):
                        for d in range(3):
                            add_to(total, (n, d, q, h), scale[b] * block_of(force, b, q, d, h))
                    add_to(total8, (n, q, h), SS[e + 1, 3] * block8_of(force, 1, q, h))
    for h in range(2):
        at = pl.ds(pl.multiple_of((COLS + 2 * p + h) * 8, 8), 8)
        for n in range(3):
            K8[n, at, :] = total8[n, 0, h] + to_next_z(total8[n, 1, h])
            for d in range(3):
                KS[d * 3 + n, at, :] = total[n, d, 0, h] + to_next_z(total[n, d, 1, h])


def put_halves(ref, row, rows_low, lanes, value):
    high, low = halves(value)
    ref[row : row + WIDE, lanes] = high
    ref[rows_low + row : rows_low + row + WIDE, lanes] = low


def all_to_all_rows(left, right):
    return lax.dot_general(left, right, (((1,), (1,)), ((), ())), preferred_element_type=F32)


def gram_sums(refs):
    XS, KS, X8, K8, LM = refs["XS"], refs["KS"], refs["X8"], refs["K8"], refs["LM"]
    GX, GY = refs["GX"], refs["GY"]
    GY[...] = jnp.zeros(GY.shape, BF16)

    def folded(width):
        out = all_to_all_rows(GX[:, 0:width], GY[:, 0:width])
        rows = out[0:WIDE] + out[WIDE : 2 * WIDE]
        return rows[:, 0:128] + rows[:, 128:256]

    def own(i, total):
        d, n = i // 2, i % 2
        for y in range(8):
            lanes = slice(y * 128, y * 128 + 128)
            rows = pl.ds(y, WIDE, stride=8)
            value = XS[d * 3 + n, rows, :]
            put_halves(GX, 0, WIDE, lanes, value)
            put_halves(GY, 0, 128, lanes, KS[d * 3 + n, rows, :])
            put_halves(GY, WIDE, 128, lanes, value * LM[n, 0, y : y + 1])
        return total + folded(1024)

    total = lax.fori_loop(0, 6, own, jnp.zeros((WIDE, 128), F32))
    GY[...] = jnp.zeros(GY.shape, BF16)

    def rim(d, total):
        for y in range(8):
            lanes = slice(y * 128, y * 128 + 128)
            rows = pl.ds(y, WIDE, stride=8)
            put_halves(GX, 0, WIDE, lanes, XS[d * 3 + 2, rows, :])
            put_halves(GY, 0, 128, lanes, KS[d * 3 + 2, rows, :])
        return total + folded(1024)

    total = lax.fori_loop(0, 3, rim, total)
    for n in range(3):
        for d in range(3):
            lanes = slice((n * 3 + d) * 128, (n * 3 + d) * 128 + 128)
            rows = pl.ds(d, WIDE, stride=8)
            put_halves(GX, 0, WIDE, lanes, X8[n, rows, :])
            put_halves(GY, 0, 128, lanes, K8[n, rows, :])
    refs["pay"][...] = total + folded(1152)


def compute(refs):
    prepare_fields(refs)

    def one(p, carry):
        current_pair(refs, p)
        previous_pair(refs, p)
        return carry

    lax.fori_loop(0, PAIRS, one, 0)

    def two(p, carry):
        second_pair(refs, p)
        return carry

    lax.fori_loop(0, 3 * PAIRS, two, 0)
    gram_sums(refs)


def compute_kernel(names, *args):
    compute(dict(zip(names, args)))


COMPUTE_SCRATCH = {
    "SS": ((4, 4, 8, 128), F32),
    "LM": ((3, 2, 8, 128), F32),
    "PM": ((3, 3, 8, 128), F32),
    "P8": ((3, 8, 128), F32),
    "VV": ((2, 3, 2, 5, 16, 128), F32),
    "UH": ((5, 96, 256), BF16),
    "UL": ((5, 96, 256), BF16),
    "U2H": ((3 * PAIRS, 3, 96, 256), BF16),
    "U2L": ((3 * PAIRS, 3, 96, 256), BF16),
    "XS": ((9, WIDE * 8, 128), F32),
    "KS": ((9, WIDE * 8, 128), F32),
    "X8": ((3, WIDE * 8, 128), F32),
    "K8": ((3, WIDE * 8, 128), F32),
    "GX": ((2 * WIDE, 1152), BF16),
    "GY": ((256, 1152), BF16),
}


def reduce_groups(sizes):
    nx, ny = sizes
    near = min(4, nx)
    groups = [("bx", 1, near), ("bx", near, nx // near), ("by", 1, ny)]
    return [g for g in groups if g[2] > 1]


def peers_of(axis, stride, size):
    at = lax.axis_index(axis)
    place = (at // stride) % size
    base = at - place * stride
    return place, [(lax.rem(place + k, size), base + lax.rem(place + k, size) * stride) for k in range(1, size)]


def greet_reducers(sizes, barrier):
    count = 0
    for axis, stride, size in reduce_groups(sizes):
        for _, peer in peers_of(axis, stride, size)[1]:
            pl.semaphore_signal(barrier, inc=1, device_id={axis: peer}, device_id_type=MESH)
            count += 1
    pl.semaphore_signal(
        barrier, inc=1, device_id={"real": 1 - lax.axis_index("real")}, device_id_type=MESH
    )
    return count + 1


def reduce_and_finish(sizes, dofs, refs):
    groups = reduce_groups(sizes)
    value = refs["pay"][...]
    for i, (axis, stride, size) in enumerate(groups):
        slots = refs[f"slots{i}"]
        place, peers = peers_of(axis, stride, size)
        slots[place] = value
        copies = []
        for k, (there, peer) in enumerate(peers):
            copies.append(
                pltpu.make_async_remote_copy(
                    src_ref=slots.at[place],
                    dst_ref=slots.at[place],
                    send_sem=refs[f"rsend{i}"].at[k],
                    recv_sem=refs[f"rrecv{i}"].at[place],
                    device_id={axis: peer},
                    device_id_type=MESH,
                )
            )
        for copy in copies:
            copy.start()
        for there, peer in peers:
            pltpu.make_async_remote_copy(
                src_ref=slots.at[place],
                dst_ref=slots.at[there],
                send_sem=refs[f"rsend{i}"].at[0],
                recv_sem=refs[f"rrecv{i}"].at[there],
                device_id={axis: peer},
                device_id_type=MESH,
            ).wait_recv()
        value = slots[0]
        for k in range(1, size):
            value = value + slots[k]
        for copy in copies:
            copy.wait_send()
    value = value / dofs
    stiff, mass = value, pltpu.roll(value, 128 - WIDE, 1)
    lane, row = lane_of(value), row_of(value)
    diagonal = (lane == row) & (row < COLS)
    stiff_diag = jnp.where(diagonal, stiff, 0.0)
    mass_diag = jnp.where(diagonal, mass, 0.0)
    quotient_col = jnp.sum(stiff_diag, axis=1, keepdims=True) / jnp.sum(
        jnp.where(diagonal, mass, jnp.where((lane == 0) & (row >= COLS), 1.0, 0.0)),
        axis=1,
        keepdims=True,
    )
    denominator_col = jnp.sum(mass_diag, axis=1, keepdims=True)
    quotient_row = jnp.sum(
        jnp.where((lane == row) & (row < COLS), quotient_col, 0.0), axis=0, keepdims=True
    )
    shifted_row = pltpu.roll(jnp.broadcast_to(quotient_row, (8, 128)), COLS, 1)[0:1]
    wide_col = jnp.broadcast_to(quotient_col, (WIDE, 128))
    shifted_col = pltpu.roll(wide_col, COLS, 0)
    for name, gram in (("gram_stiff", stiff), ("gram_mass", mass)):
        moved = pltpu.roll(gram, 128 - COLS, 1)
        side = jnp.where(
            lane < COLS, gram, jnp.where(lane < 2 * COLS, gram - shifted_row * moved, moved)
        )
        moved = pltpu.roll(side, WIDE - COLS, 0)
        full = jnp.where(
            row < COLS, side, jnp.where(row < 2 * COLS, side - shifted_col * moved, moved)
        )
        refs[name][0] = full[0 : 3 * COLS, 0 : 3 * COLS]
    weights, power_sum = [], jnp.zeros((1, 1), F32)
    for j in range(COLS):
        quotient = quotient_col[j : j + 1, 0:1]
        inverse = 1.0 / quotient
        square = inverse * inverse
        powered = square * square
        power_sum = power_sum + powered
        weights.append((quotient, powered / denominator_col[j : j + 1, 0:1]))
    terms = refs["terms"]
    for n in range(2):
        stiff_sum = jnp.zeros((8, 128), F32)
        mass_sum = jnp.zeros((8, 128), F32)
        for j, (quotient, weight) in enumerate(weights):
            stiff_sum = stiff_sum + weight * refs["ES"][j, n]
            mass_sum = mass_sum + (weight * quotient) * refs["EM"][j, n]
        terms[0, n] = (
            3.0 * refs["FE"][0, 0, n + 1, 0:8] * stiff_sum
            - refs["FE"][0, 1, n + 1, 0:8] * mass_sum
        )
    terms[0, 2] = jnp.broadcast_to(power_sum, (8, 128))
    real = lax.axis_index("real")
    swap = pltpu.make_async_remote_copy(
        src_ref=terms.at[0],
        dst_ref=terms.at[1],
        send_sem=refs["swap_sem"].at[0],
        recv_sem=refs["swap_sem"].at[1],
        device_id={"real": 1 - real},
        device_id_type=MESH,
    )
    swap.start()
    for j, (quotient, _) in enumerate(weights):
        for d in range(3):
            for n in range(2):
                refs["search"][0, j, d, n] = refs["first"][j, d, n] - quotient * refs["second"][j, d, n]
    swap.wait()
    overall = terms[0, 2] + terms[1, 2]
    for n in range(2):
        whole = (terms[0, n] + terms[1, n]) / overall
        upper = pltpu.roll(whole, 64, 1)
        refs["sens"][n] = jnp.where(real == 0, whole, upper)[:, 0:64]


def finish_kernel(sizes, dofs, names, *args):
    refs = dict(zip(names, args))
    barrier = pltpu.get_barrier_semaphore()
    count = greet_reducers(sizes, barrier)
    pl.semaphore_wait(barrier, count)
    reduce_and_finish(sizes, dofs, refs)


def reduce_scratch(sizes):
    out = {}
    for i, (_, _, size) in enumerate(reduce_groups(sizes)):
        out[f"slots{i}"] = pltpu.VMEM((size, WIDE, 128), F32)
        out[f"rsend{i}"] = pltpu.SemaphoreType.DMA((size,))
        out[f"rrecv{i}"] = pltpu.SemaphoreType.DMA((size,))
    out["terms"] = pltpu.VMEM((2, 3, 8, 128), F32)
    out["swap_sem"] = pltpu.SemaphoreType.DMA((2,))
    return out


VMEM_SPEC = pl.BlockSpec(memory_space=pltpu.VMEM)
ANY_SPEC = pl.BlockSpec(memory_space=pl.ANY)


def run(kernel, statics, ins, outs, scratch, specs=None, collective_id=None):
    names = [*ins, *outs, *scratch]
    params = dict(vmem_limit_bytes=60 * 2**20)
    if collective_id is not None:
        params.update(collective_id=collective_id, has_side_effects=True)
    result = pl.pallas_call(
        functools.partial(kernel, *statics, names),
        out_shape=[jax.ShapeDtypeStruct(shape, dtype) for shape, dtype in outs.values()],
        in_specs=[(specs or {}).get(name, VMEM_SPEC) for name in ins],
        out_specs=[VMEM_SPEC for _ in outs],
        scratch_shapes=list(scratch.values()),
        compiler_params=pltpu.CompilerParams(**params),
        name=kernel.__name__,
    )(*ins.values())
    return dict(zip(outs, result))


def shards(sizes, current, previous, element_stiffness, preconditioner, modulus, density, solid, clamped):
    size_x, size_y, size_z = modulus.shape
    nx, ny = sizes
    dofs = 3.0 * size_x * size_y * size_z * nx * ny
    bottom = (jnp.arange(size_z) == 0).astype(F32)
    keep = 1.0 - clamped.astype(F32)[:, :, None] * bottom
    share = solid[0].astype(F32)
    fields = jnp.stack(
        [
            modulus * (0.02 + 0.98 * share),
            density * (0.1 + 0.9 * share),
            keep,
            preconditioner[0, 0],
            preconditioner[0, 1],
            preconditioner[0, 2],
        ],
        0,
    ).reshape(2, 3, size_x, size_y, size_z)
    pick_row, pick_col, allow = operator_tables()
    halo = run(
        halo_kernel,
        (sizes,),
        dict(
            cur=current[0],
            prev=previous[0],
            fld=fields,
            elem=element_stiffness,
            pick_row=jnp.asarray(pick_row),
            pick_col=jnp.asarray(pick_col),
            allow=jnp.asarray(allow),
        ),
        dict(
            XC=((COLS, 3, 5, 16, 128), F32),
            XP=((COLS, 3, 3, 16, 128), F32),
            FE=((2, 3, 5, 16, 128), F32),
            WH=((2, 128, 192), BF16),
            WL=((2, 128, 192), BF16),
        ),
        dict(
            send_sem=pltpu.SemaphoreType.DMA((N_HALO,)),
            recv_sem=pltpu.SemaphoreType.DMA((N_HALO,)),
            local_sem=pltpu.SemaphoreType.DMA((3,)),
        ),
        specs=dict(cur=ANY_SPEC, prev=ANY_SPEC, fld=ANY_SPEC),
        collective_id=1,
    )
    local = run(
        compute_kernel,
        (),
        halo,
        dict(
            pay=((WIDE, 128), F32),
            first=((COLS, 3, 2, 8, 128), F32),
            second=((COLS, 3, 2, 8, 128), F32),
            ES=((COLS, 2, 8, 128), F32),
            EM=((COLS, 2, 8, 128), F32),
        ),
        {name: pltpu.VMEM(shape, dtype) for name, (shape, dtype) in COMPUTE_SCRATCH.items()},
    )
    done = run(
        finish_kernel,
        (sizes, dofs),
        dict(**local, FE=halo["FE"]),
        dict(
            gram_stiff=((1, 3 * COLS, 3 * COLS), F32),
            gram_mass=((1, 3 * COLS, 3 * COLS), F32),
            search=((1, COLS, 3, 2, 8, 128), F32),
            sens=((2, 8, 64), F32),
        ),
        reduce_scratch(sizes),
        collective_id=2,
    )
    return done["gram_stiff"], done["gram_mass"], done["search"], done["sens"]


def solution(mesh):
    sizes = (mesh.shape["bx"], mesh.shape["by"])
    return jax.shard_map(
        functools.partial(shards, sizes),
        mesh=mesh,
        in_specs=(
            P("real", None, None, "bx", "by", None),
            P("real", None, None, "bx", "by", None),
            P(),
            P("real", None, "bx", "by", None),
            P("bx", "by", None),
            P("bx", "by", None),
            P("real", "bx", "by", None),
            P("bx", "by"),
        ),
        out_specs=(
            P("real", None, None),
            P("real", None, None),
            P("real", None, None, "bx", "by", None),
            P("bx", "by", "real"),
        ),
        check_vma=False,
    )
```

```python
import functools

import jax
import jax.numpy as jnp
import numpy as np
from jax import lax
from jax.experimental import pallas as pl
from jax.experimental.pallas import tpu as pltpu
from jax.sharding import PartitionSpec as P

MESH = pl.DeviceIdType.MESH
F32 = jnp.float32
BF16 = jnp.bfloat16
COLS = 12
WIDE = 4 * COLS
PAIRS = COLS // 2
CHUNKS = 3
PER_CHUNK = COLS // CHUNKS
NOWHERE = 1000.0
DIRS = [
    (1, 0, (0, 2), (0, 8), 3, 0),
    (-1, 0, (1, 1), (0, 8), 0, 0),
    (1, 1, (0, 2), (0, 2), 3, 8),
    (1, -1, (0, 2), (7, 1), 3, 10),
    (-1, 1, (1, 1), (0, 2), 0, 8),
    (-1, -1, (1, 1), (7, 1), 0, 10),
    (0, 1, (0, 2), (0, 2), 1, 8),
    (0, -1, (0, 2), (7, 1), 1, 10),
]
PREV_DIRS = [
    (1, 0, (0, 1), (0, 8), 2, 0),
    (1, 1, (0, 1), (0, 1), 2, 8),
    (0, 1, (0, 2), (0, 1), 0, 8),
]
N_DIRS = len(DIRS)
N_HALO = N_DIRS * (1 + CHUNKS) + len(PREV_DIRS)


def operator_tables():
    out = []
    for bits in ((0, 1), (1,)):
        half = 96 + 16 * len(bits)
        pick_row = np.zeros((2 * half, 25), np.float32)
        pick_row[:, 24] = -NOWHERE
        for a in range(2):
            for b in range(2):
                for q in range(2):
                    for d in range(3):
                        i = 3 * (4 * a + 2 * b + q) + d
                        for y in range(8):
                            m = a * half + ((b * 2 + q) * 3 + d) * 8 + y
                            pick_row[m, i], pick_row[m, 24] = 1, y - b
                        if b in bits:
                            m = a * half + 96 + (bits.index(b) * 2 + q) * 8 + d
                            pick_row[m, i], pick_row[m, 24] = 1, 8 - b
        out.append(pick_row)
    first, second = [], []
    for a in range(2):
        for d in range(3):
            for q in range(2):
                for row in range(16):
                    first.append((a, d, q, -1 if row == 10 else row if row < 10 else None))
        for planes in ([(0, 0), (1, 0)], [(0, 1), (1, 1)], [(2, 0), (2, 1)]):
            for d, q in planes:
                second += [(a, d, q, y) for y in range(8)]
        for q in range(2):
            second += [(a, d % 3, q, 8 if d < 3 else None) for d in range(8)]
    for rows in (first, second):
        size = 3 * len(rows)
        pick_col = np.zeros((24, 2 * size), np.float32)
        row_y = np.full((8, size), NOWHERE * 2, np.float32)
        for part in range(3):
            for k, (a, d, q, y) in enumerate(rows):
                if y is None:
                    continue
                at = part * len(rows) + k
                row_y[:, at] = y
                for b in range(2):
                    pick_col[3 * (4 * a + 2 * b + q) + d, b * size + at] = 1
        out += [pick_col, row_y]
    row1, row2, col1, y1, col2, y2 = out
    tables = dict(
        rows=np.concatenate([row1, row2]), cols=np.concatenate([col1, col2], 1), ys=np.concatenate([y1, y2], 1)
    )
    return tables


def exact_dot(left, right):
    return lax.dot_general(
        left,
        right,
        (((1,), (0,)), ((), ())),
        preferred_element_type=F32,
        precision=lax.Precision.HIGHEST,
    )


def halves(value):
    high = value.astype(BF16)
    return high, (value - high.astype(F32)).astype(BF16)


def lane_of(value):
    return lax.broadcasted_iota(jnp.int32, value.shape, 1)


def row_of(value):
    return lax.broadcasted_iota(jnp.int32, value.shape, 0)


def from_next_z(value):
    return jnp.where(lane_of(value) == 127, 0.0, pltpu.roll(value, 127, 1))


def to_next_z(value):
    return jnp.where(lane_of(value) == 0, 0.0, pltpu.roll(value, 1, 1))


def spread(row):
    return jnp.broadcast_to(row, (8, 128))


def from_lower_y(main, below):
    return jnp.where(row_of(main) == 0, spread(below), pltpu.roll(main, 1, 0))


def from_upper_y(main, above):
    return jnp.where(row_of(main) == 7, spread(above), pltpu.roll(main, 7, 0))


def stacked_rows(rows):
    out = jnp.zeros((8, 128), F32)
    at = row_of(out)
    for d, row in enumerate(rows):
        out = jnp.where(at == d, spread(row), out)
    return out


def column_rows(index):
    return pl.ds(pl.multiple_of(index * 8, 8), 8)


class Halo:
    def __init__(self, sizes, refs):
        self.refs = refs
        self.bx, self.by = lax.axis_index("bx"), lax.axis_index("by")
        self.nx, self.ny = sizes

    def inside(self, dx, dy):
        x, y = self.bx + dx, self.by + dy
        return (x >= 0) & (x < self.nx) & (y >= 0) & (y < self.ny)

    def copy(self, source, target, job, at):
        dx, dy, (x0, xn), (y0, yn), tx, ty = job
        return pltpu.make_async_remote_copy(
            src_ref=source.at[:, :, x0 : x0 + xn, y0 : y0 + yn, :],
            dst_ref=target.at[:, :, tx : tx + xn, ty : ty + yn, :],
            send_sem=self.refs["send_sem"].at[at],
            recv_sem=self.refs["recv_sem"].at[at],
            device_id={"bx": self.bx - dx, "by": self.by - dy},
            device_id_type=MESH,
        )

    def fields(self):
        FE = self.refs["FE"]
        own = FE.at[:, :, 1:3, 0:8, :]
        return [(job, self.copy(own, FE, job, k)) for k, job in enumerate(DIRS)]

    def chunk(self, c):
        part = pl.ds(c * PER_CHUNK, PER_CHUNK)
        source, target = self.refs["cur"].at[part], self.refs["XC"].at[part]
        return [
            (job, self.copy(source, target, job, (c + 1) * N_DIRS + k))
            for k, job in enumerate(DIRS)
        ]

    def previous(self):
        first = N_DIRS * (1 + CHUNKS)
        return [
            (job, self.copy(self.refs["prev"], self.refs["XP"], job, first + k))
            for k, job in enumerate(PREV_DIRS)
        ]

    def start(self, copies):
        for job, copy in copies:
            pl.when(self.inside(-job[0], -job[1]))(copy.start)

    def arrived(self, copies):
        for job, copy in copies:
            pl.when(self.inside(job[0], job[1]))(copy.wait_recv)

    def left(self, copies):
        for job, copy in copies:
            pl.when(self.inside(-job[0], -job[1]))(copy.wait_send)

    def greet(self, barrier):
        count = 0
        for dx in (-1, 0, 1):
            for dy in (-1, 0, 1):
                if dx == 0 and dy == 0:
                    continue
                there = self.inside(dx, dy)

                @pl.when(there)
                def _():
                    pl.semaphore_signal(
                        barrier,
                        inc=1,
                        device_id={"bx": self.bx + dx, "by": self.by + dy},
                        device_id_type=MESH,
                    )

                count = count + there.astype(jnp.int32)
        return count


def own_fields(refs):
    FE = refs["FE"]
    shape = (8, 128)
    lane = lax.broadcasted_iota(jnp.int32, shape, 1)
    row = lax.broadcasted_iota(jnp.int32, shape, 0)
    for x in range(2):
        share = refs["solid_in"][x].astype(F32)
        FE[0, 0, x + 1, 0:8] = refs["modulus_in"][x] * (0.02 + 0.98 * share)
        FE[0, 1, x + 1, 0:8] = refs["density_in"][x] * (0.1 + 0.9 * share)
        held = jnp.broadcast_to(refs["clamped_in"][x : x + 1].astype(F32), (8, 8))
        held = jnp.where(
            lax.broadcasted_iota(jnp.int32, (8, 8), 0) == lax.broadcasted_iota(jnp.int32, (8, 8), 1),
            held,
            0.0,
        )
        held = jnp.sum(held, axis=1, keepdims=True)
        FE[0, 2, x + 1, 0:8] = 1.0 - jnp.where(lane == 0, held, 0.0)


def build_operators(refs):
    for row, rows, at, out in ((0, 256, 0, "W1"), (256, 224, 576, "W2")):
        table = refs["rows_in"][row : row + rows]
        size = refs[out].shape[1]
        both = exact_dot(
            exact_dot(table[:, 0:24], refs["elem_in"][...]),
            refs["cols_in"][:, 2 * at : 2 * (at + size)],
        )
        gap = refs["ys_in"][0:1, at : at + size] - table[:, 24:25]
        full = jnp.where(gap == 0.0, both[:, 0:size], 0.0) + jnp.where(
            gap == 1.0, both[:, size : 2 * size], 0.0
        )
        high = full.astype(BF16).astype(F32)
        refs[out][...] = jnp.where(lane_of(full) < 2 * size // 3, high, full - high).astype(BF16)


def prepare_fields(refs):
    FE, SS, LM, PM, P8 = refs["FE"], refs["SS"], refs["LM"], refs["PM"], refs["P8"]
    mass_sum = []
    for e in range(4):
        for kind in range(2):
            main, row8 = FE[0, kind, e, 0:8], FE[0, kind, e, 8:9]
            below = FE[0, kind, e, 10:11]
            lower = from_lower_y(main, below)
            here8, lower8 = spread(row8), spread(main[7:8])
            if kind == 0:
                SS[e, 0], SS[e, 1], SS[e, 2], SS[e, 3] = main, lower, here8, lower8
                SS[e, 4] = jnp.where(row_of(lower) == 0, 0.0, lower)
            else:
                mass_sum.append((main + lower, here8 + lower8))
    for n in range(3):
        for part in range(2):
            total = mass_sum[n][part] + mass_sum[n + 1][part]
            keep = FE[0, 2, n + 1, 0:8] if part == 0 else spread(FE[0, 2, n + 1, 8:9])
            LM[n, part] = (total + to_next_z(total)) * 0.125 * keep
        for d in range(3):
            PM[n, d] = FE[1, d, n + 1, 0:8] * FE[0, 2, n + 1, 0:8]
        P8[n] = stacked_rows([FE[1, d, n + 1, 8:9] * FE[0, 2, n + 1, 8:9] for d in range(3)])


def forces(weights, high, low):
    stacked = jnp.concatenate([high, low, high], 0)
    return lax.dot_general(
        weights, stacked, (((1,), (0,)), ((), ())), preferred_element_type=F32
    )


def block_of(force, row, h):
    return force[row : row + 8, h * 128 : h * 128 + 128]


def add_to(store, key, value):
    store[key] = value if key not in store else store[key] + value


def store_halves(high_ref, low_ref, lead, row, h, value):
    high, low = halves(value)
    at = (*lead, slice(row, row + 16), slice(h * 128, h * 128 + 128))
    high_ref[at] = high
    low_ref[at] = low


def store_second(refs, lead, h, planes, edge):
    moved = [from_next_z(plane) for plane in planes]
    blocks = [
        (planes[0], planes[1]),
        (moved[0], moved[1]),
        (planes[2], moved[2]),
        (edge, from_next_z(edge)),
    ]
    for k, block in enumerate(blocks):
        store_halves(refs["U2H"], refs["U2L"], lead, k * 16, h, jnp.concatenate(block, 0))


def current_pair(refs, p):
    XC, FE, VV, UH, UL = refs["XC"], refs["FE"], refs["VV"], refs["UH"], refs["UL"]
    SS, LM, PM, P8 = refs["SS"], refs["LM"], refs["PM"], refs["P8"]
    XS, KS, X8, K8 = refs["XS"], refs["KS"], refs["X8"], refs["K8"]
    edge = {}
    for h in range(2):
        for x in range(5):
            keep = FE[0, 2, x]
            rows = []
            for d in range(3):
                value = XC[2 * p + h, d, x] * keep
                moved = from_next_z(value)
                store_halves(UH, UL, (x,), (d * 2) * 16, h, value)
                store_halves(UH, UL, (x,), (d * 2 + 1) * 16, h, moved)
                if 1 <= x <= 3:
                    VV[h, d, 0, x - 1] = value
                    VV[h, d, 1, x - 1] = moved
                rows.append(value[8:9])
            if 1 <= x <= 3:
                edge[h, 0, x] = stacked_rows(rows)
                edge[h, 1, x] = from_next_z(edge[h, 0, x])
    total, total8, energy, energy8 = {}, {}, {}, {}
    for e in range(4):
        high = UH[e : e + 2].reshape(192, 256)
        low = UL[e : e + 2].reshape(192, 256)
        used = [a for a in range(2) if 0 <= e - 1 + a <= 2]
        force = forces(refs["W1"][used[0] * 128 : used[-1] * 128 + 128, :], high, low)
        for a in used:
            n = e - 1 + a
            start = (a - used[0]) * 128
            for h in range(2):
                for b in range(2):
                    for q in range(2):
                        for d in range(3):
                            block = block_of(force, start + ((b * 2 + q) * 3 + d) * 8, h)
                            add_to(total, (n, d, q, h), SS[e, b] * block)
                            if e in (1, 2):
                                add_to(energy, (e, b, h), VV[h, d, q, e + a - 1, 0:8] * block)
                        block = block_of(force, start + 96 + (b * 2 + q) * 8, h)
                        add_to(total8, (n, q, h), SS[e, 2 + b] * block)
                        if e in (1, 2) and b == 1:
                            add_to(energy8, (e, h), edge[h, q, e + a] * block)
    zero = jnp.zeros((8, 128), F32)
    for h in range(2):
        c = 2 * p + h
        for n in range(3):
            stiff8 = total8[n, 0, h] + to_next_z(total8[n, 1, h])
            first8 = P8[n] * stiff8
            second8 = P8[n] * LM[n, 1] * edge[h, 0, n + 1]
            for ref, col, value in (
                (X8, 0, edge[h, 0, n + 1]),
                (X8, 1, first8),
                (X8, 2, second8),
                (K8, 0, zero),
            ):
                ref[n, column_rows(col * COLS + c), :] = value
            firsts, seconds = [], []
            for d in range(3):
                stiff = total[n, d, 0, h] + to_next_z(total[n, d, 1, h])
                here = VV[h, d, 0, n, 0:8]
                firsts.append(PM[n, d] * stiff)
                seconds.append(PM[n, d] * LM[n, 0] * here)
                for ref, col, value in (
                    (XS, 0, here),
                    (XS, 1, firsts[d]),
                    (XS, 2, seconds[d]),
                    (KS, 0, stiff if n < 2 else zero),
                ):
                    ref[d * 3 + n, column_rows(col * COLS + c), :] = value
                if n < 2:
                    refs["first"][c, d, n] = firsts[d]
                    refs["second"][c, d, n] = seconds[d]
            store_second(refs, (p, n), h, firsts, first8)
            store_second(refs, (PAIRS + p, n), h, seconds, second8)
        for e in (1, 2):
            above = jnp.sum(energy8[e, h], axis=0, keepdims=True)
            refs["ES"][c, e - 1] = energy[e, 0, h] + from_upper_y(energy[e, 1, h], above)
            square = 0.0
            for x in (e - 1, e):
                for d in range(3):
                    for q in range(2):
                        square = square + VV[h, d, q, x] * VV[h, d, q, x]
            main = square[0:8]
            refs["EM"][c, e - 1] = (main + from_upper_y(main, square[8:9])) * 0.125


def previous_pair(refs, p):
    for h in range(2):
        c = 2 * p + h
        at = column_rows(3 * COLS + c)
        for n in range(3):
            rows, planes = [], []
            for d in range(3):
                value = refs["XP"][c, d, n] * refs["FE"][0, 2, n + 1]
                planes.append(value[0:8])
                refs["XS"][d * 3 + n, at, :] = planes[d]
                rows.append(value[8:9])
            edge = stacked_rows(rows)
            refs["X8"][n, at, :] = edge
            store_second(refs, (2 * PAIRS + p, n), h, planes, edge)


def second_pair(refs, p):
    SS, KS, K8 = refs["SS"], refs["KS"], refs["K8"]
    total, total8 = {}, {}
    for e in range(2):
        high = refs["U2H"][p, e : e + 2].reshape(128, 256)
        low = refs["U2L"][p, e : e + 2].reshape(128, 256)
        force = forces(refs["W2"][...], high, low)
        for a in range(2):
            n = e + a
            for h in range(2):
                for q in range(2):
                    for b in range(2):
                        for d in range(3):
                            block = block_of(force, a * 112 + ((b * 2 + q) * 3 + d) * 8, h)
                            add_to(total, (n, d, q, h), SS[e + 1, 4 * b] * block)
                    add_to(
                        total8, (n, q, h), SS[e + 1, 3] * block_of(force, a * 112 + 96 + q * 8, h)
                    )
    for h in range(2):
        at = column_rows(COLS + 2 * p + h)
        for n in range(3):
            K8[n, at, :] = total8[n, 0, h] + to_next_z(total8[n, 1, h])
            for d in range(3):
                KS[d * 3 + n, at, :] = total[n, d, 0, h] + to_next_z(total[n, d, 1, h])


def put_halves(ref, row, rows_low, lanes, value):
    high, low = halves(value)
    ref[row : row + WIDE, lanes] = high
    ref[rows_low + row : rows_low + row + WIDE, lanes] = low


def gram_sums(refs):
    XS, KS, X8, K8, LM = refs["XS"], refs["KS"], refs["X8"], refs["K8"], refs["LM"]
    GX, GY, FT = refs["GX"], refs["GY"], refs["FT"]

    def product(slot, width):
        return lax.dot_general(
            GX[slot, :, 0:width],
            GY[slot, :, 0:width],
            (((1,), (1,)), ((), ())),
            preferred_element_type=F32,
        )

    total = jnp.zeros((2 * WIDE, 4 * WIDE), F32)
    for i in range(6):
        d, n = i // 2, i % 2
        for y in range(8):
            lanes = slice(y * 128, y * 128 + 128)
            rows = pl.ds(y, WIDE, stride=8)
            value = XS[d * 3 + n, rows, :]
            put_halves(GX.at[i % 2], 0, WIDE, lanes, value)
            put_halves(GY.at[i % 2], 0, 2 * WIDE, lanes, KS[d * 3 + n, rows, :])
            put_halves(GY.at[i % 2], WIDE, 2 * WIDE, lanes, value * LM[n, 0, y : y + 1])
        total = total + product(i % 2, 1024)
    for slot in range(2):
        GY[slot] = jnp.zeros(GY.shape[1:], BF16)
    for d in range(3):
        for y in range(8):
            lanes = slice(y * 128, y * 128 + 128)
            rows = pl.ds(y, WIDE, stride=8)
            put_halves(GX.at[d % 2], 0, WIDE, lanes, XS[d * 3 + 2, rows, :])
            put_halves(GY.at[d % 2], 0, 2 * WIDE, lanes, KS[d * 3 + 2, rows, :])
        total = total + product(d % 2, 1024)
    for n in range(3):
        for d in range(3):
            lanes = slice((n * 3 + d) * 128, (n * 3 + d) * 128 + 128)
            rows = pl.ds(d, WIDE, stride=8)
            put_halves(GX.at[1], 0, WIDE, lanes, X8[n, rows, :])
            put_halves(GY.at[1], 0, 2 * WIDE, lanes, K8[n, rows, :])
    total = total + product(1, 1152)
    FT[...] = jnp.zeros(FT.shape, F32)
    FT[:, 0 : 4 * WIDE] = total[0:WIDE] + total[WIDE : 2 * WIDE]
    wide = FT[...]
    stiff = wide[:, 0:128] + pltpu.roll(wide, 256 - 2 * WIDE, 1)[:, 0:128]
    mass = pltpu.roll(stiff, 128 - WIDE, 1)
    lane, row = lane_of(stiff), row_of(stiff)
    packed = jnp.where(row >= lane, stiff, mass)
    diagonal = jnp.sum(jnp.where(row == lane, mass, 0.0), axis=1, keepdims=True)
    half = WIDE // 2
    lane = lane[0:half]
    out = jnp.where(lane < WIDE, packed[0:half], pltpu.roll(packed[half:WIDE], WIDE, 1))
    out = jnp.where(lane < 2 * WIDE, out, 0.0)
    out = jnp.where(lane == 2 * WIDE, diagonal[0:half], out)
    return jnp.where(lane == 2 * WIDE + 1, diagonal[half:WIDE], out)


COMPUTE_SCRATCH = {
    "XC": ((COLS, 3, 5, 16, 128), F32),
    "XP": ((COLS, 3, 3, 16, 128), F32),
    "FE": ((2, 3, 5, 16, 128), F32),
    "modulus_in": ((2, 8, 128), F32),
    "density_in": ((2, 8, 128), F32),
    "solid_in": ((2, 8, 128), jnp.int32),
    "clamped_in": ((2, 8), jnp.int32),
    "elem_in": ((24, 24), F32),
    "rows_in": ((480, 25), F32),
    "cols_in": ((24, 1920), F32),
    "ys_in": ((8, 960), F32),
    "W1": ((256, 576), BF16),
    "W2": ((224, 384), BF16),
    "SS": ((4, 5, 8, 128), F32),
    "LM": ((3, 2, 8, 128), F32),
    "PM": ((3, 3, 8, 128), F32),
    "P8": ((3, 8, 128), F32),
    "VV": ((2, 3, 2, 3, 16, 128), F32),
    "UH": ((5, 96, 256), BF16),
    "UL": ((5, 96, 256), BF16),
    "U2H": ((3 * PAIRS, 3, 64, 256), BF16),
    "U2L": ((3 * PAIRS, 3, 64, 256), BF16),
    "XS": ((9, WIDE * 8, 128), F32),
    "KS": ((9, WIDE * 8, 128), F32),
    "X8": ((3, WIDE * 8, 128), F32),
    "K8": ((3, WIDE * 8, 128), F32),
    "GX": ((2, 2 * WIDE, 1152), BF16),
    "GY": ((2, 4 * WIDE, 1152), BF16),
    "FT": ((WIDE, 256), F32),
    "ES": ((COLS, 2, 8, 128), F32),
    "EM": ((COLS, 2, 8, 128), F32),
}


def reduce_groups(sizes):
    nx, ny = sizes
    near = min(4, nx)
    groups = [("bx", 1, near), ("bx", near, nx // near), ("by", 1, ny)]
    return [g for g in groups if g[2] > 1]


def peers_of(axis, stride, size):
    at = lax.axis_index(axis)
    place = (at // stride) % size
    base = at - place * stride
    peers = [lax.rem(place + k, size) for k in range(1, size)]
    return place, [(there, base + there * stride) for there in peers]


def greet_reducers(sizes, barrier):
    count = 0
    for axis, stride, size in reduce_groups(sizes):
        for _, peer in peers_of(axis, stride, size)[1]:
            pl.semaphore_signal(barrier, inc=1, device_id={axis: peer}, device_id_type=MESH)
            count += 1
    pl.semaphore_signal(
        barrier, inc=1, device_id={"real": 1 - lax.axis_index("real")}, device_id_type=MESH
    )
    return count + 1


def all_reduce(sizes, refs, value):
    for i, (axis, stride, size) in enumerate(reduce_groups(sizes)):
        slots = refs[f"slots{i}"]
        place, peers = peers_of(axis, stride, size)
        slots[place] = value
        copies = [
            pltpu.make_async_remote_copy(
                src_ref=slots.at[place],
                dst_ref=slots.at[place],
                send_sem=refs[f"rsend{i}"].at[k],
                recv_sem=refs[f"rrecv{i}"].at[place],
                device_id={axis: peer},
                device_id_type=MESH,
            )
            for k, (_, peer) in enumerate(peers)
        ]
        for copy in copies:
            copy.start()
        for there, peer in peers:
            pltpu.make_async_remote_copy(
                src_ref=slots.at[place],
                dst_ref=slots.at[there],
                send_sem=refs[f"rsend{i}"].at[0],
                recv_sem=refs[f"rrecv{i}"].at[there],
                device_id={axis: peer},
                device_id_type=MESH,
            ).wait_recv()
        value = slots[0]
        for k in range(1, size):
            value = value + slots[k]
        for copy in copies:
            copy.wait_send()
    return value


def quotients(value):
    diagonal = lane_of(value) == row_of(value)
    numerator = jnp.sum(jnp.where(diagonal, value, 0.0), axis=1, keepdims=True)
    denominator = value[:, 2 * WIDE : 2 * WIDE + 1]
    return numerator / denominator, denominator


def sensitivities(refs, value):
    quotient_col, denominator_col = quotients(value)
    weights, power_sum = [], jnp.zeros((1, 1), F32)
    for j in range(COLS):
        quotient = quotient_col[j : j + 1]
        inverse = 1.0 / quotient
        square = inverse * inverse
        powered = square * square
        power_sum = power_sum + powered
        weights.append((quotient, powered / denominator_col[j : j + 1]))
    terms = refs["terms"]
    for n in range(2):
        stiff_sum = jnp.zeros((8, 128), F32)
        mass_sum = jnp.zeros((8, 128), F32)
        for j, (quotient, weight) in enumerate(weights):
            stiff_sum = stiff_sum + weight * refs["ES"][j, n]
            mass_sum = mass_sum + (weight * quotient) * refs["EM"][j, n]
        terms[0, n] = (
            3.0 * refs["FE"][0, 0, n + 1, 0:8] * stiff_sum
            - refs["FE"][0, 1, n + 1, 0:8] * mass_sum
        )
    terms[0, 2] = jnp.broadcast_to(power_sum, (8, 128))
    swap = pltpu.make_async_remote_copy(
        src_ref=terms.at[0],
        dst_ref=terms.at[1],
        send_sem=refs["swap_sem"].at[0],
        recv_sem=refs["swap_sem"].at[1],
        device_id={"real": 1 - lax.axis_index("real")},
        device_id_type=MESH,
    )
    swap.start()
    swap.wait()
    overall = terms[0, 2] + terms[1, 2]
    for n in range(2):
        refs["sens_all"][n] = (terms[0, n] + terms[1, n]) / overall


def step_kernel(sizes, dofs, names, *args):
    refs = dict(zip(names, args))
    halo = Halo(sizes, refs)
    barrier = pltpu.get_barrier_semaphore()
    FE, XC, XP, local_sem = refs["FE"], refs["XC"], refs["XP"], refs["local_sem"]
    pairs = [
        (refs["modulus"], refs["modulus_in"]),
        (refs["density"], refs["density_in"]),
        (refs["solid"].at[0], refs["solid_in"]),
        (refs["clamped"], refs["clamped_in"]),
        (refs["precond"], FE.at[1:2, :, 1:3, 0:8, :]),
        (refs["cur"], XC.at[:, :, 1:3, 0:8, :]),
        (refs["prev"], XP.at[:, :, 0:2, 0:8, :]),
        *((refs[name], refs[name + "_in"]) for name in ("elem", "rows", "cols", "ys")),
    ]
    loads = [pltpu.make_async_copy(a, b, local_sem.at[k]) for k, (a, b) in enumerate(pairs)]
    for load in loads[0:4]:
        load.start()
    for k in range(2):
        FE[k] = jnp.zeros(FE.shape[1:], F32)
    loads[4].start()
    zero_rows = jnp.zeros((3, 5, 8, 128), F32)

    def clear(c, carry):
        for x in (0, 3, 4):
            XC[c, :, x, 0:8] = jnp.zeros((3, 8, 128), F32)
        XC[c, :, :, 8:16] = zero_rows
        XP[c, :, 2, 0:8] = jnp.zeros((3, 8, 128), F32)
        XP[c, :, :, 8:16] = zero_rows[:, 0:3]
        return carry

    lax.fori_loop(0, COLS, clear, 0)
    count = halo.greet(barrier) + greet_reducers(sizes, barrier)
    for load in loads[5:]:
        load.start()
    for load in loads[0:5]:
        load.wait()
    own_fields(refs)
    pl.semaphore_wait(barrier, count)
    fields, previous = halo.fields(), halo.previous()
    halo.start(fields)
    for c in range(CHUNKS):
        halo.start(halo.chunk(c))
    halo.start(previous)
    for load in loads[5:]:
        load.wait()
    build_operators(refs)
    halo.arrived(fields)
    prepare_fields(refs)

    def one(c, carry):
        halo.arrived(halo.chunk(c))

        def inner(k, carry):
            p = c * (PER_CHUNK // 2) + k
            current_pair(refs, p)
            second_pair(refs, p)
            second_pair(refs, PAIRS + p)
            return carry

        return lax.fori_loop(0, PER_CHUNK // 2, inner, carry)

    lax.fori_loop(0, CHUNKS, one, 0)
    halo.arrived(previous)

    def two(p, carry):
        previous_pair(refs, p)
        second_pair(refs, 2 * PAIRS + p)
        return carry

    lax.fori_loop(0, PAIRS, two, 0)
    value = all_reduce(sizes, refs, gram_sums(refs)) / dofs
    refs["grams"][...] = value
    sensitivities(refs, value)
    halo.left(fields)
    for c in range(CHUNKS):
        halo.left(halo.chunk(c))
    halo.left(previous)


def result_kernel(names, *args):
    refs = dict(zip(names, args))
    value = refs["grams"][...]
    quotient_col, _ = quotients(value)
    half = WIDE // 2
    packed = jnp.concatenate([value, pltpu.roll(value, 128 - WIDE, 1)], 0)
    lane, row = lane_of(packed), row_of(packed)
    masses = jnp.concatenate(
        [value[:, 2 * WIDE : 2 * WIDE + 1], value[:, 2 * WIDE + 1 : 2 * WIDE + 2]], 0
    )
    turned = jnp.transpose(jnp.concatenate([packed, jnp.zeros((128 - WIDE, 128), F32)], 0))[0:WIDE]
    stiff = jnp.where(row >= lane, packed, turned)
    mass = jnp.where(row == lane, masses, jnp.where(row > lane, turned, packed))
    wide_col = jnp.broadcast_to(quotient_col, (half, 128))
    wide_col = jnp.concatenate([wide_col, wide_col], 0)
    on_diagonal = jnp.where((lane == row) & (row < COLS), wide_col, 0.0)
    quotient_row = jnp.broadcast_to(jnp.sum(on_diagonal, axis=0, keepdims=True), (WIDE, 128))
    shifted_row = pltpu.roll(quotient_row, COLS, 1)
    shifted_col = pltpu.roll(wide_col, COLS, 0)
    for name, gram in (("gram_stiff", stiff), ("gram_mass", mass)):
        moved = pltpu.roll(gram, 128 - COLS, 1)
        side = jnp.where(
            lane < COLS, gram, jnp.where(lane < 2 * COLS, gram - shifted_row * moved, moved)
        )
        moved = pltpu.roll(side, WIDE - COLS, 0)
        full = jnp.where(
            row < COLS, side, jnp.where(row < 2 * COLS, side - shifted_col * moved, moved)
        )
        for i in range(3 * COLS):
            refs[name][i] = full[i : i + 1, 0 : 3 * COLS]
    for j in range(COLS):
        quotient = quotient_col[j : j + 1]
        for d in range(3):
            for n in range(2):
                refs["search"][0, j, d, n] = (
                    refs["first"][j, d, n] - quotient * refs["second"][j, d, n]
                )
    real = lax.axis_index("real")
    for n in range(2):
        whole = refs["sens_all"][n]
        refs["sens"][n] = jnp.where(real == 0, whole, pltpu.roll(whole, 64, 1))[:, 0:64]


VMEM_SPEC = pl.BlockSpec(memory_space=pltpu.VMEM)
HBM_SPEC = pl.BlockSpec(memory_space=pltpu.HBM)


def run(kernel, statics, ins, outs, scratch, in_hbm=False, **params):
    names = [*ins, *outs, *scratch]
    result = pl.pallas_call(
        functools.partial(kernel, *statics, names),
        out_shape=[jax.ShapeDtypeStruct(shape, dtype) for shape, dtype in outs.values()],
        in_specs=[HBM_SPEC if in_hbm else VMEM_SPEC for name in ins],
        out_specs=[VMEM_SPEC for _ in outs],
        scratch_shapes=list(scratch.values()),
        compiler_params=pltpu.CompilerParams(**params),
        name=kernel.__name__,
    )(*(pltpu.with_memory_space_constraint(v, pltpu.HBM) if in_hbm else v for v in ins.values()))
    return dict(zip(outs, result))


def step_scratch(sizes):
    out = {name: pltpu.VMEM(shape, dtype) for name, (shape, dtype) in COMPUTE_SCRATCH.items()}
    out["send_sem"] = pltpu.SemaphoreType.DMA((N_HALO,))
    out["recv_sem"] = pltpu.SemaphoreType.DMA((N_HALO,))
    out["local_sem"] = pltpu.SemaphoreType.DMA((11,))
    for i, (_, _, size) in enumerate(reduce_groups(sizes)):
        out[f"slots{i}"] = pltpu.VMEM((size, WIDE // 2, 128), F32)
        out[f"rsend{i}"] = pltpu.SemaphoreType.DMA((size,))
        out[f"rrecv{i}"] = pltpu.SemaphoreType.DMA((size,))
    out["terms"] = pltpu.VMEM((2, 3, 8, 128), F32)
    out["swap_sem"] = pltpu.SemaphoreType.DMA((2,))
    return out


def shards(sizes, current, previous, element_stiffness, preconditioner, modulus, density, solid, clamped):
    size_x, size_y, size_z = modulus.shape
    nx, ny = sizes
    dofs = 3.0 * size_x * size_y * size_z * nx * ny
    ins = dict(
        cur=current[0],
        prev=previous[0],
        precond=preconditioner,
        modulus=modulus,
        density=density,
        solid=solid,
        clamped=clamped,
        elem=element_stiffness,
        **{name: jnp.asarray(table) for name, table in operator_tables().items()},
    )
    step = run(
        step_kernel,
        (sizes, dofs),
        ins,
        dict(
            grams=((WIDE // 2, 128), F32),
            first=((COLS, 3, 2, 8, 128), F32),
            second=((COLS, 3, 2, 8, 128), F32),
            sens_all=((2, 8, 128), F32),
        ),
        step_scratch(sizes),
        in_hbm=True,
        vmem_limit_bytes=32 * 2**20,
        collective_id=1,
        has_side_effects=True,
    )
    done = run(
        result_kernel,
        (),
        step,
        dict(
            gram_stiff=((3 * COLS, 1, 3 * COLS), F32),
            gram_mass=((3 * COLS, 1, 3 * COLS), F32),
            search=((1, COLS, 3, 2, 8, 128), F32),
            sens=((2, 8, 64), F32),
        ),
        {},
        vmem_limit_bytes=8 * 2**20,
    )
    grams = [jnp.transpose(done[name], (1, 0, 2)) for name in ("gram_stiff", "gram_mass")]
    return *grams, done["search"], done["sens"]


def solution(mesh):
    sizes = (mesh.shape["bx"], mesh.shape["by"])
    return jax.shard_map(
        functools.partial(shards, sizes),
        mesh=mesh,
        in_specs=(
            P("real", None, None, "bx", "by", None),
            P("real", None, None, "bx", "by", None),
            P(),
            P("real", None, "bx", "by", None),
            P("bx", "by", None),
            P("bx", "by", None),
            P("real", "bx", "by", None),
            P("bx", "by"),
        ),
        out_specs=(
            P("real", None, None),
            P("real", None, None),
            P("real", None, None, "bx", "by", None),
            P("bx", "by", "real"),
        ),
        check_vma=False,
    )
```

```python
import functools

import jax
import jax.numpy as jnp
import numpy as np
from jax import lax
from jax.experimental import pallas as pl
from jax.experimental.pallas import tpu as pltpu
from jax.sharding import PartitionSpec as P

MESH = pl.DeviceIdType.MESH
F32 = jnp.float32
BF16 = jnp.bfloat16
COLS = 12
WIDE = 4 * COLS
PAIRS = COLS // 2
CHUNKS = 3
PER_CHUNK = COLS // CHUNKS
NOWHERE = 1000.0
DIRS = [
    (1, 0, (0, 2), (0, 8), 3, 0),
    (-1, 0, (1, 1), (0, 8), 0, 0),
    (1, 1, (0, 2), (0, 2), 3, 8),
    (1, -1, (0, 2), (7, 1), 3, 10),
    (-1, 1, (1, 1), (0, 2), 0, 8),
    (-1, -1, (1, 1), (7, 1), 0, 10),
    (0, 1, (0, 2), (0, 2), 1, 8),
    (0, -1, (0, 2), (7, 1), 1, 10),
]
PREV_DIRS = [
    (1, 0, (0, 1), (0, 8), 2, 0),
    (1, 1, (0, 1), (0, 1), 2, 8),
    (0, 1, (0, 2), (0, 1), 0, 8),
]
N_DIRS = len(DIRS)
N_HALO = N_DIRS * (1 + CHUNKS) + len(PREV_DIRS)


def operator_tables():
    out = []
    for bits in ((0, 1), (1,)):
        half = 96 + 16 * len(bits)
        pick_row = np.zeros((2 * half, 25), np.float32)
        pick_row[:, 24] = -NOWHERE
        for a in range(2):
            for b in range(2):
                for q in range(2):
                    for d in range(3):
                        i = 3 * (4 * a + 2 * b + q) + d
                        for y in range(8):
                            m = a * half + ((b * 2 + q) * 3 + d) * 8 + y
                            pick_row[m, i], pick_row[m, 24] = 1, y - b
                        if b in bits:
                            m = a * half + 96 + (bits.index(b) * 2 + q) * 8 + d
                            pick_row[m, i], pick_row[m, 24] = 1, 8 - b
        out.append(pick_row)
    first, second = [], []
    for a in range(2):
        for d in range(3):
            for q in range(2):
                for row in range(16):
                    first.append((a, d, q, -1 if row == 10 else row if row < 10 else None))
        for planes in ([(0, 0), (1, 0)], [(0, 1), (1, 1)], [(2, 0), (2, 1)]):
            for d, q in planes:
                second += [(a, d, q, y) for y in range(8)]
        for q in range(2):
            second += [(a, d % 3, q, 8 if d < 3 else None) for d in range(8)]
    for rows in (first, second):
        size = 3 * len(rows)
        pick_col = np.zeros((48, 2 * size), np.float32)
        row_y = np.full((8, size), NOWHERE * 2, np.float32)
        for part in range(3):
            for k, (a, d, q, y) in enumerate(rows):
                if y is None:
                    continue
                at = part * len(rows) + k
                row_y[:, at] = y
                for b in range(2):
                    i = 24 * (part == 2) + 3 * (4 * a + 2 * b + q) + d
                    pick_col[i, b * size + at] = 1
        out += [pick_col, row_y]
    row1, row2, col1, y1, col2, y2 = out
    rows = np.concatenate([row1, row2])
    return dict(
        rows=rows[:, 0:24],
        row_ys=np.tile(rows[:, 24:25], (1, 128)),
        cols=np.concatenate([col1, col2], 1),
        col_ys=np.concatenate([y1, y2], 1),
    )


def pick_dot(left, right):
    return lax.dot_general(left, right, (((1,), (0,)), ((), ())), preferred_element_type=F32)


def halves(value):
    high = value.astype(BF16)
    return high, (value - high.astype(F32)).astype(BF16)


def lane_of(value):
    return lax.broadcasted_iota(jnp.int32, value.shape, 1)


def row_of(value):
    return lax.broadcasted_iota(jnp.int32, value.shape, 0)


def from_next_z(value):
    return jnp.where(lane_of(value) == 127, 0.0, pltpu.roll(value, 127, 1))


def to_next_z(value):
    return jnp.where(lane_of(value) == 0, 0.0, pltpu.roll(value, 1, 1))


def spread(row):
    return jnp.broadcast_to(row, (8, 128))


def from_lower_y(main, below):
    return jnp.where(row_of(main) == 0, spread(below), pltpu.roll(main, 1, 0))


def from_upper_y(main, above):
    return jnp.where(row_of(main) == 7, spread(above), pltpu.roll(main, 7, 0))


def stacked_rows(rows):
    out = jnp.zeros((8, 128), F32)
    at = row_of(out)
    for d, row in enumerate(rows):
        out = jnp.where(at == d, spread(row), out)
    return out


def column_rows(index):
    return pl.ds(index, 8, stride=WIDE)


class Halo:
    def __init__(self, sizes, refs):
        self.refs = refs
        self.bx, self.by = lax.axis_index("bx"), lax.axis_index("by")
        self.nx, self.ny = sizes

    def inside(self, dx, dy):
        x, y = self.bx + dx, self.by + dy
        return (x >= 0) & (x < self.nx) & (y >= 0) & (y < self.ny)

    def copy(self, source, target, job, at):
        dx, dy, (x0, xn), (y0, yn), tx, ty = job
        return pltpu.make_async_remote_copy(
            src_ref=source.at[:, :, x0 : x0 + xn, y0 : y0 + yn, :],
            dst_ref=target.at[:, :, tx : tx + xn, ty : ty + yn, :],
            send_sem=self.refs["send_sem"].at[at],
            recv_sem=self.refs["recv_sem"].at[at],
            device_id={"bx": self.bx - dx, "by": self.by - dy},
            device_id_type=MESH,
        )

    def fields(self):
        FE = self.refs["FE"]
        own = FE.at[:, :, 1:3, 0:8, :]
        return [(job, self.copy(own, FE, job, k)) for k, job in enumerate(DIRS)]

    def chunk(self, c):
        part = pl.ds(c * PER_CHUNK, PER_CHUNK)
        source, target = self.refs["cur"].at[part], self.refs["XC"].at[part]
        return [
            (job, self.copy(source, target, job, (c + 1) * N_DIRS + k))
            for k, job in enumerate(DIRS)
        ]

    def previous(self):
        first = N_DIRS * (1 + CHUNKS)
        return [
            (job, self.copy(self.refs["prev"], self.refs["XP"], job, first + k))
            for k, job in enumerate(PREV_DIRS)
        ]

    def start(self, copies):
        for job, copy in copies:
            pl.when(self.inside(-job[0], -job[1]))(copy.start)

    def arrived(self, copies):
        for job, copy in copies:
            pl.when(self.inside(job[0], job[1]))(copy.wait_recv)

    def left(self, copies):
        for job, copy in copies:
            pl.when(self.inside(-job[0], -job[1]))(copy.wait_send)

    def greet(self, barrier):
        count = 0
        for dx in (-1, 0, 1):
            for dy in (-1, 0, 1):
                if dx == 0 and dy == 0:
                    continue
                there = self.inside(dx, dy)

                @pl.when(there)
                def _():
                    pl.semaphore_signal(
                        barrier,
                        inc=1,
                        device_id={"bx": self.bx + dx, "by": self.by + dy},
                        device_id_type=MESH,
                    )

                count = count + there.astype(jnp.int32)
        return count


def own_fields(refs):
    FE = refs["FE"]
    shape = (8, 128)
    lane = lax.broadcasted_iota(jnp.int32, shape, 1)
    row = lax.broadcasted_iota(jnp.int32, shape, 0)
    for x in range(2):
        share = refs["solid_in"][x].astype(F32)
        FE[0, 0, x + 1, 0:8] = refs["modulus_in"][x] * (0.02 + 0.98 * share)
        FE[0, 1, x + 1, 0:8] = refs["density_in"][x] * (0.1 + 0.9 * share)
        held = jnp.broadcast_to(refs["clamped_in"][x : x + 1].astype(F32), (8, 8))
        held = jnp.where(
            lax.broadcasted_iota(jnp.int32, (8, 8), 0) == lax.broadcasted_iota(jnp.int32, (8, 8), 1),
            held,
            0.0,
        )
        held = jnp.sum(held, axis=1, keepdims=True)
        FE[0, 2, x + 1, 0:8] = 1.0 - jnp.where(lane == 0, held, 0.0)


def build_operators(refs):
    high, low = halves(refs["elem_in"][...])
    spread_high = pick_dot(refs["rows_in"][...], high).astype(BF16)
    spread_low = pick_dot(refs["rows_in"][...], low).astype(BF16)
    for row, rows, at, out in ((0, 256, 0, "W1"), (256, 224, 576, "W2")):
        size = refs[out].shape[1]
        cols = refs["cols_in"]
        gap = refs["col_ys_in"][0:1, at : at + size]
        total = 0.0
        for b in range(2):
            columns = slice(2 * at + b * size, 2 * at + (b + 1) * size)
            picked = pick_dot(spread_high[row : row + rows], cols[0:24, columns]) + pick_dot(
                spread_low[row : row + rows], cols[24:48, columns]
            )
            match = gap - refs["row_ys_in"][row : row + rows, 0:1] == float(b)
            total = total + jnp.where(match, picked, 0.0)
        refs[out][...] = total.astype(BF16)


def prepare_fields(refs):
    FE, SS, LM, PM, P8 = refs["FE"], refs["SS"], refs["LM"], refs["PM"], refs["P8"]
    mass_sum = []
    for e in range(4):
        for kind in range(2):
            main, row8 = FE[0, kind, e, 0:8], FE[0, kind, e, 8:9]
            below = FE[0, kind, e, 10:11]
            lower = from_lower_y(main, below)
            here8, lower8 = spread(row8), spread(main[7:8])
            if kind == 0:
                SS[e, 0], SS[e, 1], SS[e, 2], SS[e, 3] = main, lower, here8, lower8
                SS[e, 4] = jnp.where(row_of(lower) == 0, 0.0, lower)
            else:
                mass_sum.append((main + lower, here8 + lower8))
    for n in range(3):
        for part in range(2):
            total = mass_sum[n][part] + mass_sum[n + 1][part]
            keep = FE[0, 2, n + 1, 0:8] if part == 0 else spread(FE[0, 2, n + 1, 8:9])
            LM[n, part] = (total + to_next_z(total)) * 0.125 * keep
        for d in range(3):
            PM[n, d] = FE[1, d, n + 1, 0:8] * FE[0, 2, n + 1, 0:8]
        P8[n] = stacked_rows([FE[1, d, n + 1, 8:9] * FE[0, 2, n + 1, 8:9] for d in range(3)])


def forces(weights, high, low):
    stacked = jnp.concatenate([high, low, high], 0)
    return lax.dot_general(
        weights, stacked, (((1,), (0,)), ((), ())), preferred_element_type=F32
    )


def block_of(force, row, h):
    return force[row : row + 8, h * 128 : h * 128 + 128]


def add_to(store, key, value):
    store[key] = value if key not in store else store[key] + value


def store_halves(high_ref, low_ref, lead, row, h, value):
    high, low = halves(value)
    at = (*lead, slice(row, row + 16), slice(h * 128, h * 128 + 128))
    high_ref[at] = high
    low_ref[at] = low


def store_second(refs, lead, h, planes, edge):
    moved = [from_next_z(plane) for plane in planes]
    blocks = [
        (planes[0], planes[1]),
        (moved[0], moved[1]),
        (planes[2], moved[2]),
        (edge, from_next_z(edge)),
    ]
    for k, block in enumerate(blocks):
        store_halves(refs["U2H"], refs["U2L"], lead, k * 16, h, jnp.concatenate(block, 0))


def current_pair(refs, p):
    XC, FE, VV, UH, UL = refs["XC"], refs["FE"], refs["VV"], refs["UH"], refs["UL"]
    SS, LM, PM, P8 = refs["SS"], refs["LM"], refs["PM"], refs["P8"]
    XS, KS, X8, K8 = refs["XS"], refs["KS"], refs["X8"], refs["K8"]
    edge = {}
    for h in range(2):
        for x in range(5):
            keep = FE[0, 2, x]
            rows = []
            for d in range(3):
                value = XC[2 * p + h, d, x] * keep
                moved = from_next_z(value)
                store_halves(UH, UL, (x,), (d * 2) * 16, h, value)
                store_halves(UH, UL, (x,), (d * 2 + 1) * 16, h, moved)
                if 1 <= x <= 3:
                    VV[h, d, 0, x - 1] = value
                    VV[h, d, 1, x - 1] = moved
                rows.append(value[8:9])
            if 1 <= x <= 3:
                edge[h, 0, x] = stacked_rows(rows)
                edge[h, 1, x] = from_next_z(edge[h, 0, x])
    total, total8, energy, energy8 = {}, {}, {}, {}
    for e in range(4):
        high = UH[e : e + 2].reshape(192, 256)
        low = UL[e : e + 2].reshape(192, 256)
        used = [a for a in range(2) if 0 <= e - 1 + a <= 2]
        force = forces(refs["W1"][used[0] * 128 : used[-1] * 128 + 128, :], high, low)
        for a in used:
            n = e - 1 + a
            start = (a - used[0]) * 128
            for h in range(2):
                for b in range(2):
                    for q in range(2):
                        for d in range(3):
                            block = block_of(force, start + ((b * 2 + q) * 3 + d) * 8, h)
                            add_to(total, (n, d, q, h), SS[e, b] * block)
                            if e in (1, 2):
                                add_to(energy, (e, b, h), VV[h, d, q, e + a - 1, 0:8] * block)
                        block = block_of(force, start + 96 + (b * 2 + q) * 8, h)
                        add_to(total8, (n, q, h), SS[e, 2 + b] * block)
                        if e in (1, 2) and b == 1:
                            add_to(energy8, (e, h), edge[h, q, e + a] * block)
    zero = jnp.zeros((8, 128), F32)
    for h in range(2):
        c = 2 * p + h
        for n in range(3):
            stiff8 = total8[n, 0, h] + to_next_z(total8[n, 1, h])
            first8 = P8[n] * stiff8
            second8 = P8[n] * LM[n, 1] * edge[h, 0, n + 1]
            for ref, col, value in (
                (X8, 0, edge[h, 0, n + 1]),
                (X8, 1, first8),
                (X8, 2, second8),
                (K8, 0, zero),
            ):
                ref[n, column_rows(col * COLS + c), :] = value
            firsts, seconds = [], []
            for d in range(3):
                stiff = total[n, d, 0, h] + to_next_z(total[n, d, 1, h])
                here = VV[h, d, 0, n, 0:8]
                firsts.append(PM[n, d] * stiff)
                seconds.append(PM[n, d] * LM[n, 0] * here)
                for ref, col, value in (
                    (XS, 0, here),
                    (XS, 1, firsts[d]),
                    (XS, 2, seconds[d]),
                    (KS, 0, stiff if n < 2 else zero),
                ):
                    ref[d * 3 + n, column_rows(col * COLS + c), :] = value
                if n < 2:
                    refs["first"][c, d, n] = firsts[d]
                    refs["second"][c, d, n] = seconds[d]
            store_second(refs, (p, n), h, firsts, first8)
            store_second(refs, (PAIRS + p, n), h, seconds, second8)
        top, bottom = 0.0, 0.0
        for n in range(2):
            for d in range(3):
                here = VV[h, d, 0, n, 0:8]
                stiff = total[n, d, 0, h] + to_next_z(total[n, d, 1, h])
                top = top + here * stiff
                bottom = bottom + here * here * LM[n, 0]
        refs["QV"][pl.ds(c, 1), :] = jnp.sum(top, axis=0, keepdims=True)
        refs["QV"][pl.ds(16 + c, 1), :] = jnp.sum(bottom, axis=0, keepdims=True)
        for e in (1, 2):
            above = jnp.sum(energy8[e, h], axis=0, keepdims=True)
            refs["ES"][c, e - 1] = energy[e, 0, h] + from_upper_y(energy[e, 1, h], above)
            square = 0.0
            for x in (e - 1, e):
                for d in range(3):
                    for q in range(2):
                        square = square + VV[h, d, q, x] * VV[h, d, q, x]
            main = square[0:8]
            refs["EM"][c, e - 1] = (main + from_upper_y(main, square[8:9])) * 0.125


def previous_pair(refs, p):
    for h in range(2):
        c = 2 * p + h
        at = column_rows(3 * COLS + c)
        for n in range(3):
            rows, planes = [], []
            for d in range(3):
                value = refs["XP"][c, d, n] * refs["FE"][0, 2, n + 1]
                planes.append(value[0:8])
                refs["XS"][d * 3 + n, at, :] = planes[d]
                rows.append(value[8:9])
            edge = stacked_rows(rows)
            refs["X8"][n, at, :] = edge
            store_second(refs, (2 * PAIRS + p, n), h, planes, edge)


def second_pair(refs, p):
    SS, KS, K8 = refs["SS"], refs["KS"], refs["K8"]
    total, total8 = {}, {}
    for e in range(2):
        high = refs["U2H"][p, e : e + 2].reshape(128, 256)
        low = refs["U2L"][p, e : e + 2].reshape(128, 256)
        force = forces(refs["W2"][...], high, low)
        for a in range(2):
            n = e + a
            for h in range(2):
                for q in range(2):
                    for b in range(2):
                        for d in range(3):
                            block = block_of(force, a * 112 + ((b * 2 + q) * 3 + d) * 8, h)
                            add_to(total, (n, d, q, h), SS[e + 1, 4 * b] * block)
                    add_to(
                        total8, (n, q, h), SS[e + 1, 3] * block_of(force, a * 112 + 96 + q * 8, h)
                    )
    for h in range(2):
        at = column_rows(COLS + 2 * p + h)
        for n in range(3):
            K8[n, at, :] = total8[n, 0, h] + to_next_z(total8[n, 1, h])
            for d in range(3):
                KS[d * 3 + n, at, :] = total[n, d, 0, h] + to_next_z(total[n, d, 1, h])


def put_halves(ref, row, rows_low, lanes, value):
    high, low = halves(value)
    ref[row : row + WIDE, lanes] = high
    ref[rows_low + row : rows_low + row + WIDE, lanes] = low


def gram_sums(refs, between):
    XS, KS, X8, K8, LM = refs["XS"], refs["KS"], refs["X8"], refs["K8"], refs["LM"]
    GX, GY, FT = refs["GX"], refs["GY"], refs["FT"]

    def product(slot, width):
        return lax.dot_general(
            GX[slot, :, 0:width],
            GY[slot, :, 0:width],
            (((1,), (1,)), ((), ())),
            preferred_element_type=F32,
        )

    total = jnp.zeros((2 * WIDE, 4 * WIDE), F32)
    for i in range(6):
        d, n = i // 2, i % 2
        for y in range(8):
            lanes = slice(y * 128, y * 128 + 128)
            rows = slice(y * WIDE, (y + 1) * WIDE)
            value = XS[d * 3 + n, rows, :]
            put_halves(GX.at[i % 2], 0, WIDE, lanes, value)
            put_halves(GY.at[i % 2], 0, 2 * WIDE, lanes, KS[d * 3 + n, rows, :])
            put_halves(GY.at[i % 2], WIDE, 2 * WIDE, lanes, value * LM[n, 0, y : y + 1])
        total = total + product(i % 2, 1024)
        if i == 3:
            between()
    for slot in range(2):
        GY[slot] = jnp.zeros(GY.shape[1:], BF16)
    for d in range(3):
        for y in range(8):
            lanes = slice(y * 128, y * 128 + 128)
            rows = slice(y * WIDE, (y + 1) * WIDE)
            put_halves(GX.at[d % 2], 0, WIDE, lanes, XS[d * 3 + 2, rows, :])
            put_halves(GY.at[d % 2], 0, 2 * WIDE, lanes, KS[d * 3 + 2, rows, :])
        total = total + product(d % 2, 1024)
    for n in range(3):
        for d in range(3):
            lanes = slice((n * 3 + d) * 128, (n * 3 + d) * 128 + 128)
            rows = slice(d * WIDE, (d + 1) * WIDE)
            put_halves(GX.at[1], 0, WIDE, lanes, X8[n, rows, :])
            put_halves(GY.at[1], 0, 2 * WIDE, lanes, K8[n, rows, :])
    total = total + product(1, 1152)
    FT[...] = jnp.zeros(FT.shape, F32)
    FT[:, 0 : 4 * WIDE] = total[0:WIDE] + total[WIDE : 2 * WIDE]
    wide = FT[...]
    stiff = wide[:, 0:128] + pltpu.roll(wide, 256 - 2 * WIDE, 1)[:, 0:128]
    mass = pltpu.roll(stiff, 128 - WIDE, 1)
    lane, row = lane_of(stiff), row_of(stiff)
    packed = jnp.where(row >= lane, stiff, mass)
    diagonal = jnp.sum(jnp.where(row == lane, mass, 0.0), axis=1, keepdims=True)
    half = WIDE // 2
    lane = lane[0:half]
    out = jnp.where(lane < WIDE, packed[0:half], pltpu.roll(packed[half:WIDE], WIDE, 1))
    out = jnp.where(lane < 2 * WIDE, out, 0.0)
    out = jnp.where(lane == 2 * WIDE, diagonal[0:half], out)
    return jnp.where(lane == 2 * WIDE + 1, diagonal[half:WIDE], out)


COMPUTE_SCRATCH = {
    "XC": ((COLS, 3, 5, 16, 128), F32),
    "XP": ((COLS, 3, 3, 16, 128), F32),
    "FE": ((2, 3, 5, 16, 128), F32),
    "modulus_in": ((2, 8, 128), F32),
    "density_in": ((2, 8, 128), F32),
    "solid_in": ((2, 8, 128), jnp.int32),
    "clamped_in": ((2, 8), jnp.int32),
    "elem_in": ((24, 24), F32),
    "rows_in": ((480, 24), BF16),
    "row_ys_in": ((480, 128), F32),
    "cols_in": ((48, 1920), BF16),
    "col_ys_in": ((8, 960), F32),
    "W1": ((256, 576), BF16),
    "W2": ((224, 384), BF16),
    "SS": ((4, 5, 8, 128), F32),
    "LM": ((3, 2, 8, 128), F32),
    "PM": ((3, 3, 8, 128), F32),
    "P8": ((3, 8, 128), F32),
    "VV": ((2, 3, 2, 3, 16, 128), F32),
    "UH": ((5, 96, 256), BF16),
    "UL": ((5, 96, 256), BF16),
    "U2H": ((3 * PAIRS, 3, 64, 256), BF16),
    "U2L": ((3 * PAIRS, 3, 64, 256), BF16),
    "XS": ((9, WIDE * 8, 128), F32),
    "KS": ((9, WIDE * 8, 128), F32),
    "X8": ((3, WIDE * 8, 128), F32),
    "K8": ((3, WIDE * 8, 128), F32),
    "GX": ((2, 2 * WIDE, 1152), BF16),
    "GY": ((2, 4 * WIDE, 1152), BF16),
    "FT": ((WIDE, 256), F32),
    "QV": ((32, 128), F32),
    "ES": ((COLS, 2, 8, 128), F32),
    "EM": ((COLS, 2, 8, 128), F32),
}


def reduce_groups(sizes):
    nx, ny = sizes
    groups = [("bx", 1, 2), ("bx", 2, nx // 2), ("by", 1, ny)]
    return [g for g in groups if g[2] > 1]


def peers_of(axis, stride, size):
    at = lax.axis_index(axis)
    place = (at // stride) % size
    base = at - place * stride
    peers = [lax.rem(place + k, size) for k in range(1, size)]
    return place, [(there, base + there * stride) for there in peers]


def greet_reducers(sizes, barrier):
    count = 0
    for axis, stride, size in reduce_groups(sizes):
        for _, peer in peers_of(axis, stride, size)[1]:
            pl.semaphore_signal(barrier, inc=1, device_id={axis: peer}, device_id_type=MESH)
            count += 1
    pl.semaphore_signal(
        barrier, inc=1, device_id={"real": 1 - lax.axis_index("real")}, device_id_type=MESH
    )
    return count + 1


class Reducer:
    def __init__(self, sizes, refs, tag):
        self.refs, self.tag, self.groups = refs, tag, reduce_groups(sizes)

    def part(self, name, i):
        return self.refs[f"{name}{self.tag}{i}"]

    def copy(self, i, place, slot, peer, k):
        return pltpu.make_async_remote_copy(
            src_ref=self.part("slots", i).at[place],
            dst_ref=self.part("slots", i).at[slot],
            send_sem=self.part("rsend", i).at[k],
            recv_sem=self.part("rrecv", i).at[slot],
            device_id={self.groups[i][0]: peer},
            device_id_type=MESH,
        )

    def start(self, i, value):
        place, peers = peers_of(*self.groups[i])
        self.part("slots", i)[place] = value
        for k, (_, peer) in enumerate(peers):
            self.copy(i, place, place, peer, k).start()

    def end(self, i):
        place, peers = peers_of(*self.groups[i])
        for k, (there, peer) in enumerate(peers):
            self.copy(i, place, there, peer, k).wait_recv()
        slots = self.part("slots", i)
        value = slots[0]
        for k in range(1, self.groups[i][2]):
            value = value + slots[k]
        return value

    def sent(self):
        for i, group in enumerate(self.groups):
            place, peers = peers_of(*group)
            for k, (_, peer) in enumerate(peers):
                self.copy(i, place, place, peer, k).wait_send()


def quotients(sums):
    sums = jnp.sum(sums, axis=1, keepdims=True)
    return sums[0:16] / sums[16:32], sums[16:32]


def send_sensitivities(refs, dofs, sums):
    quotient_col, denominator_col = quotients(sums)
    denominator_col = denominator_col / dofs
    weights, power_sum = [], jnp.zeros((1, 1), F32)
    for j in range(COLS):
        quotient = quotient_col[j : j + 1]
        inverse = 1.0 / quotient
        square = inverse * inverse
        powered = square * square
        power_sum = power_sum + powered
        weights.append((quotient, powered / denominator_col[j : j + 1]))
    terms = refs["terms"]
    for n in range(2):
        stiff_sum = jnp.zeros((8, 128), F32)
        mass_sum = jnp.zeros((8, 128), F32)
        for j, (quotient, weight) in enumerate(weights):
            stiff_sum = stiff_sum + weight * refs["ES"][j, n]
            mass_sum = mass_sum + (weight * quotient) * refs["EM"][j, n]
        terms[0, n] = (
            3.0 * refs["FE"][0, 0, n + 1, 0:8] * stiff_sum
            - refs["FE"][0, 1, n + 1, 0:8] * mass_sum
        )
    terms[0, 2] = jnp.broadcast_to(power_sum, (8, 128))
    swap_of(refs).start()


def swap_of(refs):
    return pltpu.make_async_remote_copy(
        src_ref=refs["terms"].at[0],
        dst_ref=refs["terms"].at[1],
        send_sem=refs["swap_sem"].at[0],
        recv_sem=refs["swap_sem"].at[1],
        device_id={"real": 1 - lax.axis_index("real")},
        device_id_type=MESH,
    )


def end_sensitivities(refs):
    swap_of(refs).wait()
    terms = refs["terms"]
    overall = terms[0, 2] + terms[1, 2]
    for n in range(2):
        refs["sens_all"][n] = (terms[0, n] + terms[1, n]) / overall


def step_kernel(sizes, dofs, names, *args):
    refs = dict(zip(names, args))
    halo = Halo(sizes, refs)
    barrier = pltpu.get_barrier_semaphore()
    FE, XC, XP, local_sem = refs["FE"], refs["XC"], refs["XP"], refs["local_sem"]
    pairs = [
        (refs["modulus"], refs["modulus_in"]),
        (refs["density"], refs["density_in"]),
        (refs["solid"].at[0], refs["solid_in"]),
        (refs["clamped"], refs["clamped_in"]),
        (refs["precond"], FE.at[1:2, :, 1:3, 0:8, :]),
        (refs["cur"], XC.at[:, :, 1:3, 0:8, :]),
        (refs["prev"], XP.at[:, :, 0:2, 0:8, :]),
        *((refs[name], refs[name + "_in"]) for name in ("elem", "rows", "row_ys", "cols", "col_ys")),
    ]
    loads = [pltpu.make_async_copy(a, b, local_sem.at[k]) for k, (a, b) in enumerate(pairs)]
    for load in loads[0:4]:
        load.start()
    count = greet_reducers(sizes, barrier)
    refs["QV"][...] = jnp.zeros((32, 128), F32)
    for k in range(2):
        FE[k] = jnp.zeros(FE.shape[1:], F32)
    loads[4].start()
    zero_rows = jnp.zeros((3, 5, 8, 128), F32)

    def clear(c, carry):
        for x in (0, 3, 4):
            XC[c, :, x, 0:8] = jnp.zeros((3, 8, 128), F32)
        XC[c, :, :, 8:16] = zero_rows
        XP[c, :, 2, 0:8] = jnp.zeros((3, 8, 128), F32)
        XP[c, :, :, 8:16] = zero_rows[:, 0:3]
        return carry

    lax.fori_loop(0, COLS, clear, 0)
    count = count + halo.greet(barrier)
    for load in loads[5:]:
        load.start()
    for load in loads[0:5]:
        load.wait()
    own_fields(refs)
    pl.semaphore_wait(barrier, count)
    fields, previous = halo.fields(), halo.previous()
    halo.start(fields)
    halo.start(halo.chunk(0))
    halo.start(previous)

    def send(c, carry):
        halo.start(halo.chunk(c))
        return carry

    lax.fori_loop(1, CHUNKS, send, 0)
    for load in loads[5:]:
        load.wait()
    build_operators(refs)
    halo.arrived(fields)
    prepare_fields(refs)

    def earlier(p, carry):
        previous_pair(refs, p)
        second_pair(refs, 2 * PAIRS + p)
        return carry

    halo.arrived(halo.chunk(0))
    current_pair(refs, 0)

    def one(p, carry):
        @pl.when(p == PER_CHUNK // 2)
        def _():
            halo.arrived(previous)
            lax.fori_loop(0, PAIRS, earlier, 0)

        @pl.when(p % (PER_CHUNK // 2) == 0)
        def _():
            halo.arrived(halo.chunk(p // (PER_CHUNK // 2)))

        second_pair(refs, p - 1)
        second_pair(refs, PAIRS + p - 1)
        current_pair(refs, p)
        return carry

    lax.fori_loop(1, PAIRS, one, 0)
    second_pair(refs, PAIRS - 1)
    second_pair(refs, 2 * PAIRS - 1)
    early, late = Reducer(sizes, refs, "q"), Reducer(sizes, refs, "g")
    stages = len(early.groups)
    early.start(0, refs["QV"][...])

    def between():
        early.start(1, early.end(0))

    late.start(0, gram_sums(refs, between))
    for i in range(1, stages):
        late.start(i, late.end(i - 1))
        sums = early.end(i)
        if i + 1 < stages:
            early.start(i + 1, sums)
    refs["sums"][...] = sums
    send_sensitivities(refs, dofs, sums)
    refs["grams"][...] = late.end(stages - 1) / dofs
    end_sensitivities(refs)
    early.sent()
    late.sent()
    halo.left(fields)
    halo.left(previous)

    def sent(c, carry):
        halo.left(halo.chunk(c))
        return carry

    lax.fori_loop(0, CHUNKS, sent, 0)


def result_kernel(names, *args):
    refs = dict(zip(names, args))
    value = refs["grams"][...]
    quotient_col, _ = quotients(refs["sums"][...])
    packed = jnp.concatenate([value, pltpu.roll(value, 128 - WIDE, 1)], 0)
    lane, row = lane_of(packed), row_of(packed)
    masses = jnp.concatenate(
        [value[:, 2 * WIDE : 2 * WIDE + 1], value[:, 2 * WIDE + 1 : 2 * WIDE + 2]], 0
    )
    turned = jnp.transpose(jnp.concatenate([packed, jnp.zeros((128 - WIDE, 128), F32)], 0))[0:WIDE]
    stiff = jnp.where(row >= lane, packed, turned)
    mass = jnp.where(row == lane, masses, jnp.where(row > lane, turned, packed))
    wide_col = jnp.broadcast_to(quotient_col, (16, 128))
    wide_col = jnp.concatenate([wide_col, wide_col, wide_col], 0)
    on_diagonal = jnp.where((lane == row) & (row < COLS), wide_col, 0.0)
    quotient_row = jnp.broadcast_to(jnp.sum(on_diagonal, axis=0, keepdims=True), (WIDE, 128))
    shifted_row = pltpu.roll(quotient_row, COLS, 1)
    shifted_col = pltpu.roll(wide_col, COLS, 0)
    for name, gram in (("gram_stiff", stiff), ("gram_mass", mass)):
        moved = pltpu.roll(gram, 128 - COLS, 1)
        side = jnp.where(
            lane < COLS, gram, jnp.where(lane < 2 * COLS, gram - shifted_row * moved, moved)
        )
        moved = pltpu.roll(side, WIDE - COLS, 0)
        full = jnp.where(
            row < COLS, side, jnp.where(row < 2 * COLS, side - shifted_col * moved, moved)
        )
        for i in range(3 * COLS):
            refs[name][i] = full[i : i + 1, 0 : 3 * COLS]
    for j in range(COLS):
        quotient = quotient_col[j : j + 1]
        for d in range(3):
            for n in range(2):
                refs["search"][0, j, d, n] = (
                    refs["first"][j, d, n] - quotient * refs["second"][j, d, n]
                )
    real = lax.axis_index("real")
    for n in range(2):
        whole = refs["sens_all"][n]
        refs["sens"][n] = jnp.where(real == 0, whole, pltpu.roll(whole, 64, 1))[:, 0:64]


VMEM_SPEC = pl.BlockSpec(memory_space=pltpu.VMEM)
HBM_SPEC = pl.BlockSpec(memory_space=pltpu.HBM)


def run(kernel, statics, ins, outs, scratch, in_hbm=False, **params):
    names = [*ins, *outs, *scratch]
    result = pl.pallas_call(
        functools.partial(kernel, *statics, names),
        out_shape=[jax.ShapeDtypeStruct(shape, dtype) for shape, dtype in outs.values()],
        in_specs=[HBM_SPEC if in_hbm else VMEM_SPEC for name in ins],
        out_specs=[VMEM_SPEC for _ in outs],
        scratch_shapes=list(scratch.values()),
        compiler_params=pltpu.CompilerParams(**params),
        name=kernel.__name__,
    )(*(pltpu.with_memory_space_constraint(v, pltpu.HBM) if in_hbm else v for v in ins.values()))
    return dict(zip(outs, result))


def step_scratch(sizes):
    out = {name: pltpu.VMEM(shape, dtype) for name, (shape, dtype) in COMPUTE_SCRATCH.items()}
    out["send_sem"] = pltpu.SemaphoreType.DMA((N_HALO,))
    out["recv_sem"] = pltpu.SemaphoreType.DMA((N_HALO,))
    out["local_sem"] = pltpu.SemaphoreType.DMA((12,))
    for i, (_, _, size) in enumerate(reduce_groups(sizes)):
        for tag, rows in (("q", 32), ("g", WIDE // 2)):
            out[f"slots{tag}{i}"] = pltpu.VMEM((size, rows, 128), F32)
            out[f"rsend{tag}{i}"] = pltpu.SemaphoreType.DMA((size,))
            out[f"rrecv{tag}{i}"] = pltpu.SemaphoreType.DMA((size,))
    out["terms"] = pltpu.VMEM((2, 3, 8, 128), F32)
    out["swap_sem"] = pltpu.SemaphoreType.DMA((2,))
    return out


def shards(sizes, current, previous, element_stiffness, preconditioner, modulus, density, solid, clamped):
    size_x, size_y, size_z = modulus.shape
    nx, ny = sizes
    dofs = 3.0 * size_x * size_y * size_z * nx * ny
    ins = dict(
        cur=current[0],
        prev=previous[0],
        precond=preconditioner,
        modulus=modulus,
        density=density,
        solid=solid,
        clamped=clamped,
        elem=element_stiffness,
        **{
            name: jnp.asarray(table, COMPUTE_SCRATCH[name + "_in"][1])
            for name, table in operator_tables().items()
        },
    )
    step = run(
        step_kernel,
        (sizes, dofs),
        ins,
        dict(
            grams=((WIDE // 2, 128), F32),
            sums=((32, 128), F32),
            first=((COLS, 3, 2, 8, 128), F32),
            second=((COLS, 3, 2, 8, 128), F32),
            sens_all=((2, 8, 128), F32),
        ),
        step_scratch(sizes),
        in_hbm=True,
        vmem_limit_bytes=32 * 2**20,
        collective_id=1,
        has_side_effects=True,
    )
    done = run(
        result_kernel,
        (),
        step,
        dict(
            gram_stiff=((3 * COLS, 1, 3 * COLS), F32),
            gram_mass=((3 * COLS, 1, 3 * COLS), F32),
            search=((1, COLS, 3, 2, 8, 128), F32),
            sens=((2, 8, 64), F32),
        ),
        {},
        vmem_limit_bytes=8 * 2**20,
    )
    grams = [jnp.transpose(done[name], (1, 0, 2)) for name in ("gram_stiff", "gram_mass")]
    return *grams, done["search"], done["sens"]


def solution(mesh):
    sizes = (mesh.shape["bx"], mesh.shape["by"])
    return jax.shard_map(
        functools.partial(shards, sizes),
        mesh=mesh,
        in_specs=(
            P("real", None, None, "bx", "by", None),
            P("real", None, None, "bx", "by", None),
            P(),
            P("real", None, "bx", "by", None),
            P("bx", "by", None),
            P("bx", "by", None),
            P("real", "bx", "by", None),
            P("bx", "by"),
        ),
        out_specs=(
            P("real", None, None),
            P("real", None, None),
            P("real", None, None, "bx", "by", None),
            P("bx", "by", "real"),
        ),
        check_vma=False,
    )
```

```python
import functools

import jax
import jax.numpy as jnp
import numpy as np
from jax import lax
from jax.experimental import pallas as pl
from jax.experimental.pallas import tpu as pltpu
from jax.sharding import PartitionSpec as P

MESH = pl.DeviceIdType.MESH
F32 = jnp.float32
BF16 = jnp.bfloat16
COLS = 12
WIDE = 4 * COLS
PAIRS = COLS // 2
CHUNKS = 3
PER_CHUNK = COLS // CHUNKS
NOWHERE = 1000.0
DIRS = [
    (1, 0, (0, 2), (0, 8), 3, 0),
    (-1, 0, (1, 1), (0, 8), 0, 0),
    (1, 1, (0, 2), (0, 2), 3, 8),
    (1, -1, (0, 2), (7, 1), 3, 10),
    (-1, 1, (1, 1), (0, 2), 0, 8),
    (-1, -1, (1, 1), (7, 1), 0, 10),
    (0, 1, (0, 2), (0, 2), 1, 8),
    (0, -1, (0, 2), (7, 1), 1, 10),
]
PREV_DIRS = [
    (1, 0, (0, 1), (0, 8), 2, 0),
    (1, 1, (0, 1), (0, 1), 2, 8),
    (0, 1, (0, 2), (0, 1), 0, 8),
]
N_DIRS = len(DIRS)
N_HALO = N_DIRS * (1 + CHUNKS) + len(PREV_DIRS)


def operator_tables():
    out = []
    for bits in ((0, 1), (1,)):
        half = 96 + 16 * len(bits)
        pick_row = np.zeros((2 * half, 25), np.float32)
        pick_row[:, 24] = -NOWHERE
        for a in range(2):
            for b in range(2):
                for q in range(2):
                    for d in range(3):
                        i = 3 * (4 * a + 2 * b + q) + d
                        for y in range(8):
                            m = a * half + ((b * 2 + q) * 3 + d) * 8 + y
                            pick_row[m, i], pick_row[m, 24] = 1, y - b
                        if b in bits:
                            m = a * half + 96 + (bits.index(b) * 2 + q) * 8 + d
                            pick_row[m, i], pick_row[m, 24] = 1, 8 - b
        out.append(pick_row)
    first, second = [], []
    for a in range(2):
        for d in range(3):
            for q in range(2):
                for row in range(16):
                    first.append((a, d, q, -1 if row == 10 else row if row < 10 else None))
        for planes in ([(0, 0), (1, 0)], [(0, 1), (1, 1)], [(2, 0), (2, 1)]):
            for d, q in planes:
                second += [(a, d, q, y) for y in range(8)]
        for q in range(2):
            second += [(a, d % 3, q, 8 if d < 3 else None) for d in range(8)]
    for rows in (first, second):
        size = 3 * len(rows)
        pick_col = np.zeros((48, 2 * size), np.float32)
        row_y = np.full((8, size), NOWHERE * 2, np.float32)
        for part in range(3):
            for k, (a, d, q, y) in enumerate(rows):
                if y is None:
                    continue
                at = part * len(rows) + k
                row_y[:, at] = y
                for b in range(2):
                    i = 24 * (part == 2) + 3 * (4 * a + 2 * b + q) + d
                    pick_col[i, b * size + at] = 1
        out += [pick_col, row_y]
    row1, row2, col1, y1, col2, y2 = out
    rows = np.concatenate([row1, row2])
    return dict(
        rows=rows[:, 0:24],
        row_ys=np.tile(rows[:, 24:25], (1, 128)),
        cols=np.concatenate([col1, col2], 1),
        col_ys=np.concatenate([y1, y2], 1),
    )


def pick_dot(left, right):
    return lax.dot_general(left, right, (((1,), (0,)), ((), ())), preferred_element_type=F32)


def halves(value):
    high = value.astype(BF16)
    return high, (value - high.astype(F32)).astype(BF16)


def lane_of(value):
    return lax.broadcasted_iota(jnp.int32, value.shape, 1)


def row_of(value):
    return lax.broadcasted_iota(jnp.int32, value.shape, 0)


def from_next_z(value):
    return jnp.where(lane_of(value) == 127, 0.0, pltpu.roll(value, 127, 1))


def to_next_z(value):
    return jnp.where(lane_of(value) == 0, 0.0, pltpu.roll(value, 1, 1))


def spread(row):
    return jnp.broadcast_to(row, (8, 128))


def from_lower_y(main, below):
    return jnp.where(row_of(main) == 0, spread(below), pltpu.roll(main, 1, 0))


def from_upper_y(main, above):
    return jnp.where(row_of(main) == 7, spread(above), pltpu.roll(main, 7, 0))


def stacked_rows(rows):
    out = jnp.zeros((8, 128), F32)
    at = row_of(out)
    for d, row in enumerate(rows):
        out = jnp.where(at == d, spread(row), out)
    return out


def column_rows(index):
    return pl.ds(index, 8, stride=WIDE)


class Halo:
    def __init__(self, sizes, refs):
        self.refs = refs
        self.bx, self.by = lax.axis_index("bx"), lax.axis_index("by")
        self.nx, self.ny = sizes

    def inside(self, dx, dy):
        x, y = self.bx + dx, self.by + dy
        return (x >= 0) & (x < self.nx) & (y >= 0) & (y < self.ny)

    def copy(self, source, target, job, at):
        dx, dy, (x0, xn), (y0, yn), tx, ty = job
        return pltpu.make_async_remote_copy(
            src_ref=source.at[:, :, x0 : x0 + xn, y0 : y0 + yn, :],
            dst_ref=target.at[:, :, tx : tx + xn, ty : ty + yn, :],
            send_sem=self.refs["send_sem"].at[at],
            recv_sem=self.refs["recv_sem"].at[at],
            device_id={"bx": self.bx - dx, "by": self.by - dy},
            device_id_type=MESH,
        )

    def fields(self):
        FE = self.refs["FE"]
        own = FE.at[:, :, 1:3, 0:8, :]
        return [(job, self.copy(own, FE, job, k)) for k, job in enumerate(DIRS)]

    def chunk(self, c):
        part = pl.ds(c * PER_CHUNK, PER_CHUNK)
        source, target = self.refs["cur"].at[part], self.refs["XC"].at[part]
        return [
            (job, self.copy(source, target, job, (c + 1) * N_DIRS + k))
            for k, job in enumerate(DIRS)
        ]

    def previous(self):
        first = N_DIRS * (1 + CHUNKS)
        return [
            (job, self.copy(self.refs["prev"], self.refs["XP"], job, first + k))
            for k, job in enumerate(PREV_DIRS)
        ]

    def start(self, copies):
        for job, copy in copies:
            pl.when(self.inside(-job[0], -job[1]))(copy.start)

    def arrived(self, copies):
        for job, copy in copies:
            pl.when(self.inside(job[0], job[1]))(copy.wait_recv)

    def left(self, copies):
        for job, copy in copies:
            pl.when(self.inside(-job[0], -job[1]))(copy.wait_send)

    def greet(self, barrier):
        count = 0
        for dx in (-1, 0, 1):
            for dy in (-1, 0, 1):
                if dx == 0 and dy == 0:
                    continue
                there = self.inside(dx, dy)

                @pl.when(there)
                def _():
                    pl.semaphore_signal(
                        barrier,
                        inc=1,
                        device_id={"bx": self.bx + dx, "by": self.by + dy},
                        device_id_type=MESH,
                    )

                count = count + there.astype(jnp.int32)
        return count


def own_fields(refs):
    FE = refs["FE"]
    shape = (8, 128)
    lane = lax.broadcasted_iota(jnp.int32, shape, 1)
    row = lax.broadcasted_iota(jnp.int32, shape, 0)
    for x in range(2):
        share = refs["solid_in"][x].astype(F32)
        FE[0, 0, x + 1, 0:8] = refs["modulus_in"][x] * (0.02 + 0.98 * share)
        FE[0, 1, x + 1, 0:8] = refs["density_in"][x] * (0.1 + 0.9 * share)
        held = jnp.broadcast_to(refs["clamped_in"][x : x + 1].astype(F32), (8, 8))
        held = jnp.where(
            lax.broadcasted_iota(jnp.int32, (8, 8), 0) == lax.broadcasted_iota(jnp.int32, (8, 8), 1),
            held,
            0.0,
        )
        held = jnp.sum(held, axis=1, keepdims=True)
        FE[0, 2, x + 1, 0:8] = 1.0 - jnp.where(lane == 0, held, 0.0)


def build_operators(refs):
    high, low = halves(refs["elem_in"][...])
    spread_high = pick_dot(refs["rows_in"][...], high).astype(BF16)
    spread_low = pick_dot(refs["rows_in"][...], low).astype(BF16)
    for row, rows, at, out in ((0, 256, 0, "W1"), (256, 224, 576, "W2")):
        size = refs[out].shape[1]
        cols = refs["cols_in"]
        gap = refs["col_ys_in"][0:1, at : at + size]
        total = 0.0
        for b in range(2):
            columns = slice(2 * at + b * size, 2 * at + (b + 1) * size)
            picked = pick_dot(spread_high[row : row + rows], cols[0:24, columns]) + pick_dot(
                spread_low[row : row + rows], cols[24:48, columns]
            )
            match = gap - refs["row_ys_in"][row : row + rows, 0:1] == float(b)
            total = total + jnp.where(match, picked, 0.0)
        refs[out][...] = total.astype(BF16)


def prepare_fields(refs):
    FE, SS, LM, PM, P8 = refs["FE"], refs["SS"], refs["LM"], refs["PM"], refs["P8"]
    mass_sum = []
    for e in range(4):
        for kind in range(2):
            main, row8 = FE[0, kind, e, 0:8], FE[0, kind, e, 8:9]
            below = FE[0, kind, e, 10:11]
            lower = from_lower_y(main, below)
            here8, lower8 = spread(row8), spread(main[7:8])
            if kind == 0:
                SS[e, 0], SS[e, 1], SS[e, 2], SS[e, 3] = main, lower, here8, lower8
                SS[e, 4] = jnp.where(row_of(lower) == 0, 0.0, lower)
            else:
                mass_sum.append((main + lower, here8 + lower8))
    for n in range(3):
        for part in range(2):
            total = mass_sum[n][part] + mass_sum[n + 1][part]
            keep = FE[0, 2, n + 1, 0:8] if part == 0 else spread(FE[0, 2, n + 1, 8:9])
            LM[n, part] = (total + to_next_z(total)) * 0.125 * keep
        for d in range(3):
            PM[n, d] = FE[1, d, n + 1, 0:8] * FE[0, 2, n + 1, 0:8]
        P8[n] = stacked_rows([FE[1, d, n + 1, 8:9] * FE[0, 2, n + 1, 8:9] for d in range(3)])


def forces(weights, high, low):
    stacked = jnp.concatenate([high, low, high], 0)
    return lax.dot_general(
        weights, stacked, (((1,), (0,)), ((), ())), preferred_element_type=F32
    )


def block_of(force, row, h):
    return force[row : row + 8, h * 128 : h * 128 + 128]


def add_to(store, key, value):
    store[key] = value if key not in store else store[key] + value


def store_halves(high_ref, low_ref, lead, row, h, value):
    high, low = halves(value)
    at = (*lead, slice(row, row + 16), slice(h * 128, h * 128 + 128))
    high_ref[at] = high
    low_ref[at] = low


def store_second(refs, lead, h, planes, edge):
    moved = [from_next_z(plane) for plane in planes]
    blocks = [
        (planes[0], planes[1]),
        (moved[0], moved[1]),
        (planes[2], moved[2]),
        (edge, from_next_z(edge)),
    ]
    for k, block in enumerate(blocks):
        store_halves(refs["U2H"], refs["U2L"], lead, k * 16, h, jnp.concatenate(block, 0))


def current_pair(refs, p):
    XC, FE, VV, UH, UL = refs["XC"], refs["FE"], refs["VV"], refs["UH"], refs["UL"]
    SS, LM, PM, P8 = refs["SS"], refs["LM"], refs["PM"], refs["P8"]
    XS, KS, X8, K8 = refs["XS"], refs["KS"], refs["X8"], refs["K8"]
    edge = {}
    for h in range(2):
        for x in range(5):
            keep = FE[0, 2, x]
            rows = []
            for d in range(3):
                value = XC[2 * p + h, d, x] * keep
                moved = from_next_z(value)
                store_halves(UH, UL, (x,), (d * 2) * 16, h, value)
                store_halves(UH, UL, (x,), (d * 2 + 1) * 16, h, moved)
                if 1 <= x <= 3:
                    VV[h, d, 0, x - 1] = value
                    VV[h, d, 1, x - 1] = moved
                rows.append(value[8:9])
            if 1 <= x <= 3:
                edge[h, 0, x] = stacked_rows(rows)
                edge[h, 1, x] = from_next_z(edge[h, 0, x])
    total, total8, energy, energy8 = {}, {}, {}, {}
    for e in range(4):
        high = UH[e : e + 2].reshape(192, 256)
        low = UL[e : e + 2].reshape(192, 256)
        used = [a for a in range(2) if 0 <= e - 1 + a <= 2]
        force = forces(refs["W1"][used[0] * 128 : used[-1] * 128 + 128, :], high, low)
        for a in used:
            n = e - 1 + a
            start = (a - used[0]) * 128
            for h in range(2):
                for b in range(2):
                    for q in range(2):
                        for d in range(3):
                            block = block_of(force, start + ((b * 2 + q) * 3 + d) * 8, h)
                            add_to(total, (n, d, q, h), SS[e, b] * block)
                            if e in (1, 2):
                                add_to(energy, (e, b, h), VV[h, d, q, e + a - 1, 0:8] * block)
                        block = block_of(force, start + 96 + (b * 2 + q) * 8, h)
                        add_to(total8, (n, q, h), SS[e, 2 + b] * block)
                        if e in (1, 2) and b == 1:
                            add_to(energy8, (e, h), edge[h, q, e + a] * block)
    zero = jnp.zeros((8, 128), F32)
    for h in range(2):
        c = 2 * p + h
        for n in range(3):
            stiff8 = total8[n, 0, h] + to_next_z(total8[n, 1, h])
            first8 = P8[n] * stiff8
            second8 = P8[n] * LM[n, 1] * edge[h, 0, n + 1]
            for ref, col, value in (
                (X8, 0, edge[h, 0, n + 1]),
                (X8, 1, first8),
                (X8, 2, second8),
                (K8, 0, zero),
            ):
                ref[n, column_rows(col * COLS + c), :] = value
            firsts, seconds = [], []
            for d in range(3):
                stiff = total[n, d, 0, h] + to_next_z(total[n, d, 1, h])
                here = VV[h, d, 0, n, 0:8]
                firsts.append(PM[n, d] * stiff)
                seconds.append(PM[n, d] * LM[n, 0] * here)
                for ref, col, value in (
                    (XS, 0, here),
                    (XS, 1, firsts[d]),
                    (XS, 2, seconds[d]),
                    (KS, 0, stiff if n < 2 else zero),
                ):
                    ref[d * 3 + n, column_rows(col * COLS + c), :] = value
                if n < 2:
                    refs["first"][c, d, n] = firsts[d]
                    refs["second"][c, d, n] = seconds[d]
            store_second(refs, (p, n), h, firsts, first8)
            store_second(refs, (PAIRS + p, n), h, seconds, second8)
        top, bottom = 0.0, 0.0
        for n in range(2):
            for d in range(3):
                here = VV[h, d, 0, n, 0:8]
                stiff = total[n, d, 0, h] + to_next_z(total[n, d, 1, h])
                top = top + here * stiff
                bottom = bottom + here * here * LM[n, 0]
        refs["QV"][pl.ds(c, 1), :] = jnp.sum(top, axis=0, keepdims=True)
        refs["QV"][pl.ds(16 + c, 1), :] = jnp.sum(bottom, axis=0, keepdims=True)
        for e in (1, 2):
            above = jnp.sum(energy8[e, h], axis=0, keepdims=True)
            refs["ES"][c, e - 1] = energy[e, 0, h] + from_upper_y(energy[e, 1, h], above)
            square = 0.0
            for x in (e - 1, e):
                for d in range(3):
                    for q in range(2):
                        square = square + VV[h, d, q, x] * VV[h, d, q, x]
            main = square[0:8]
            refs["EM"][c, e - 1] = (main + from_upper_y(main, square[8:9])) * 0.125


def previous_pair(refs, p):
    for h in range(2):
        c = 2 * p + h
        at = column_rows(3 * COLS + c)
        for n in range(3):
            rows, planes = [], []
            for d in range(3):
                value = refs["XP"][c, d, n] * refs["FE"][0, 2, n + 1]
                planes.append(value[0:8])
                refs["XS"][d * 3 + n, at, :] = planes[d]
                rows.append(value[8:9])
            edge = stacked_rows(rows)
            refs["X8"][n, at, :] = edge
            store_second(refs, (2 * PAIRS + p, n), h, planes, edge)


def second_pair(refs, p):
    SS, KS, K8 = refs["SS"], refs["KS"], refs["K8"]
    total, total8 = {}, {}
    for e in range(2):
        high = refs["U2H"][p, e : e + 2].reshape(128, 256)
        low = refs["U2L"][p, e : e + 2].reshape(128, 256)
        force = forces(refs["W2"][...], high, low)
        for a in range(2):
            n = e + a
            for h in range(2):
                for q in range(2):
                    for b in range(2):
                        for d in range(3):
                            block = block_of(force, a * 112 + ((b * 2 + q) * 3 + d) * 8, h)
                            add_to(total, (n, d, q, h), SS[e + 1, 4 * b] * block)
                    add_to(
                        total8, (n, q, h), SS[e + 1, 3] * block_of(force, a * 112 + 96 + q * 8, h)
                    )
    for h in range(2):
        at = column_rows(COLS + 2 * p + h)
        for n in range(3):
            K8[n, at, :] = total8[n, 0, h] + to_next_z(total8[n, 1, h])
            for d in range(3):
                KS[d * 3 + n, at, :] = total[n, d, 0, h] + to_next_z(total[n, d, 1, h])


def put_halves(ref, row, rows_low, lanes, value):
    high, low = halves(value)
    ref[row : row + WIDE, lanes] = high
    ref[rows_low + row : rows_low + row + WIDE, lanes] = low


def gram_sums(refs, between):
    XS, KS, X8, K8, LM = refs["XS"], refs["KS"], refs["X8"], refs["K8"], refs["LM"]
    GX, GY, FT = refs["GX"], refs["GY"], refs["FT"]

    def product(slot, width):
        return lax.dot_general(
            GX[slot, :, 0:width],
            GY[slot, :, 0:width],
            (((1,), (1,)), ((), ())),
            preferred_element_type=F32,
        )

    total = jnp.zeros((2 * WIDE, 4 * WIDE), F32)
    for i in range(6):
        d, n = i // 2, i % 2
        for y in range(8):
            lanes = slice(y * 128, y * 128 + 128)
            rows = slice(y * WIDE, (y + 1) * WIDE)
            value = XS[d * 3 + n, rows, :]
            put_halves(GX.at[i % 2], 0, WIDE, lanes, value)
            put_halves(GY.at[i % 2], 0, 2 * WIDE, lanes, KS[d * 3 + n, rows, :])
            put_halves(GY.at[i % 2], WIDE, 2 * WIDE, lanes, value * LM[n, 0, y : y + 1])
        total = total + product(i % 2, 1024)
        if i == 3:
            between()
    for slot in range(2):
        GY[slot] = jnp.zeros(GY.shape[1:], BF16)
    for d in range(3):
        for y in range(8):
            lanes = slice(y * 128, y * 128 + 128)
            rows = slice(y * WIDE, (y + 1) * WIDE)
            put_halves(GX.at[d % 2], 0, WIDE, lanes, XS[d * 3 + 2, rows, :])
            put_halves(GY.at[d % 2], 0, 2 * WIDE, lanes, KS[d * 3 + 2, rows, :])
        total = total + product(d % 2, 1024)
    for n in range(3):
        for d in range(3):
            lanes = slice((n * 3 + d) * 128, (n * 3 + d) * 128 + 128)
            rows = slice(d * WIDE, (d + 1) * WIDE)
            put_halves(GX.at[1], 0, WIDE, lanes, X8[n, rows, :])
            put_halves(GY.at[1], 0, 2 * WIDE, lanes, K8[n, rows, :])
    total = total + product(1, 1152)
    FT[...] = jnp.zeros(FT.shape, F32)
    FT[:, 0 : 4 * WIDE] = total[0:WIDE] + total[WIDE : 2 * WIDE]
    wide = FT[...]
    stiff = wide[:, 0:128] + pltpu.roll(wide, 256 - 2 * WIDE, 1)[:, 0:128]
    mass = pltpu.roll(stiff, 128 - WIDE, 1)
    lane, row = lane_of(stiff), row_of(stiff)
    packed = jnp.where(row >= lane, stiff, mass)
    diagonal = jnp.sum(jnp.where(row == lane, mass, 0.0), axis=1, keepdims=True)
    half = WIDE // 2
    lane = lane[0:half]
    out = jnp.where(lane < WIDE, packed[0:half], pltpu.roll(packed[half:WIDE], WIDE, 1))
    out = jnp.where(lane < 2 * WIDE, out, 0.0)
    out = jnp.where(lane == 2 * WIDE, diagonal[0:half], out)
    return jnp.where(lane == 2 * WIDE + 1, diagonal[half:WIDE], out)


COMPUTE_SCRATCH = {
    "XC": ((COLS, 3, 5, 16, 128), F32),
    "XP": ((COLS, 3, 3, 16, 128), F32),
    "FE": ((2, 3, 5, 16, 128), F32),
    "modulus_in": ((2, 8, 128), F32),
    "density_in": ((2, 8, 128), F32),
    "solid_in": ((2, 8, 128), jnp.int32),
    "clamped_in": ((2, 8), jnp.int32),
    "elem_in": ((24, 24), F32),
    "rows_in": ((480, 24), BF16),
    "row_ys_in": ((480, 128), F32),
    "cols_in": ((48, 1920), BF16),
    "col_ys_in": ((8, 960), F32),
    "W1": ((256, 576), BF16),
    "W2": ((224, 384), BF16),
    "SS": ((4, 5, 8, 128), F32),
    "LM": ((3, 2, 8, 128), F32),
    "PM": ((3, 3, 8, 128), F32),
    "P8": ((3, 8, 128), F32),
    "VV": ((2, 3, 2, 3, 16, 128), F32),
    "UH": ((5, 96, 256), BF16),
    "UL": ((5, 96, 256), BF16),
    "U2H": ((3 * PAIRS, 3, 64, 256), BF16),
    "U2L": ((3 * PAIRS, 3, 64, 256), BF16),
    "XS": ((9, WIDE * 8, 128), F32),
    "KS": ((9, WIDE * 8, 128), F32),
    "X8": ((3, WIDE * 8, 128), F32),
    "K8": ((3, WIDE * 8, 128), F32),
    "GX": ((2, 2 * WIDE, 1152), BF16),
    "GY": ((2, 4 * WIDE, 1152), BF16),
    "FT": ((WIDE, 256), F32),
    "QV": ((32, 128), F32),
    "ES": ((COLS, 2, 8, 128), F32),
    "EM": ((COLS, 2, 8, 128), F32),
}


def reduce_groups(sizes):
    nx, ny = sizes
    groups = [("bx", 1, 2), ("bx", 2, nx // 2), ("by", 1, ny)]
    return [g for g in groups if g[2] > 1]


def peers_of(axis, stride, size):
    at = lax.axis_index(axis)
    place = (at // stride) % size
    base = at - place * stride
    peers = [lax.rem(place + k, size) for k in range(1, size)]
    return place, [(there, base + there * stride) for there in peers]


def greet_reducers(sizes, barrier):
    count = 0
    for axis, stride, size in reduce_groups(sizes):
        for _, peer in peers_of(axis, stride, size)[1]:
            pl.semaphore_signal(barrier, inc=1, device_id={axis: peer}, device_id_type=MESH)
            count += 1
    pl.semaphore_signal(
        barrier, inc=1, device_id={"real": 1 - lax.axis_index("real")}, device_id_type=MESH
    )
    return count + 1


class Reducer:
    def __init__(self, sizes, refs, tag):
        self.refs, self.tag, self.groups = refs, tag, reduce_groups(sizes)

    def part(self, name, i):
        return self.refs[f"{name}{self.tag}{i}"]

    def copy(self, i, place, slot, peer, k):
        return pltpu.make_async_remote_copy(
            src_ref=self.part("slots", i).at[place],
            dst_ref=self.part("slots", i).at[slot],
            send_sem=self.part("rsend", i).at[k],
            recv_sem=self.part("rrecv", i).at[slot],
            device_id={self.groups[i][0]: peer},
            device_id_type=MESH,
        )

    def start(self, i, value):
        place, peers = peers_of(*self.groups[i])
        self.part("slots", i)[place] = value
        for k, (_, peer) in enumerate(peers):
            self.copy(i, place, place, peer, k).start()

    def end(self, i):
        place, peers = peers_of(*self.groups[i])
        for k, (there, peer) in enumerate(peers):
            self.copy(i, place, there, peer, k).wait_recv()
        slots = self.part("slots", i)
        value = slots[0]
        for k in range(1, self.groups[i][2]):
            value = value + slots[k]
        return value

    def sent(self, stages):
        for i in stages:
            place, peers = peers_of(*self.groups[i])
            for k, (_, peer) in enumerate(peers):
                self.copy(i, place, place, peer, k).wait_send()


def quotients(sums):
    sums = jnp.sum(sums, axis=1, keepdims=True)
    return sums[0:16] / sums[16:32], sums[16:32]


def send_sensitivities(refs, dofs, sums):
    quotient_col, denominator_col = quotients(sums)
    denominator_col = denominator_col / dofs
    weights, power_sum = [], jnp.zeros((1, 1), F32)
    for j in range(COLS):
        quotient = quotient_col[j : j + 1]
        inverse = 1.0 / quotient
        square = inverse * inverse
        powered = square * square
        power_sum = power_sum + powered
        weights.append((quotient, powered / denominator_col[j : j + 1]))
    terms = refs["terms"]
    for n in range(2):
        stiff_sum = jnp.zeros((8, 128), F32)
        mass_sum = jnp.zeros((8, 128), F32)
        for j, (quotient, weight) in enumerate(weights):
            stiff_sum = stiff_sum + weight * refs["ES"][j, n]
            mass_sum = mass_sum + (weight * quotient) * refs["EM"][j, n]
        terms[0, n] = (
            3.0 * refs["FE"][0, 0, n + 1, 0:8] * stiff_sum
            - refs["FE"][0, 1, n + 1, 0:8] * mass_sum
        )
    terms[0, 2] = jnp.broadcast_to(power_sum, (8, 128))
    swap_of(refs).start()


def swap_of(refs):
    return pltpu.make_async_remote_copy(
        src_ref=refs["terms"].at[0],
        dst_ref=refs["terms"].at[1],
        send_sem=refs["swap_sem"].at[0],
        recv_sem=refs["swap_sem"].at[1],
        device_id={"real": 1 - lax.axis_index("real")},
        device_id_type=MESH,
    )


def end_sensitivities(refs):
    swap_of(refs).wait()
    terms = refs["terms"]
    overall = terms[0, 2] + terms[1, 2]
    for n in range(2):
        refs["sens_all"][n] = (terms[0, n] + terms[1, n]) / overall


def step_kernel(sizes, dofs, names, *args):
    refs = dict(zip(names, args))
    halo = Halo(sizes, refs)
    barrier = pltpu.get_barrier_semaphore()
    FE, XC, XP, local_sem = refs["FE"], refs["XC"], refs["XP"], refs["local_sem"]
    pairs = [
        (refs["modulus"], refs["modulus_in"]),
        (refs["density"], refs["density_in"]),
        (refs["solid"].at[0], refs["solid_in"]),
        (refs["clamped"], refs["clamped_in"]),
        (refs["precond"], FE.at[1:2, :, 1:3, 0:8, :]),
        (refs["cur"], XC.at[:, :, 1:3, 0:8, :]),
        (refs["prev"], XP.at[:, :, 0:2, 0:8, :]),
        *((refs[name], refs[name + "_in"]) for name in ("elem", "rows", "row_ys", "cols", "col_ys")),
    ]
    loads = [pltpu.make_async_copy(a, b, local_sem.at[k]) for k, (a, b) in enumerate(pairs)]
    for load in loads[0:4]:
        load.start()
    count = greet_reducers(sizes, barrier)
    refs["QV"][...] = jnp.zeros((32, 128), F32)
    for k in range(2):
        FE[k] = jnp.zeros(FE.shape[1:], F32)
    loads[4].start()
    zero_rows = jnp.zeros((3, 5, 8, 128), F32)

    def clear(c, carry):
        for x in (0, 3, 4):
            XC[c, :, x, 0:8] = jnp.zeros((3, 8, 128), F32)
        XC[c, :, :, 8:16] = zero_rows
        XP[c, :, 2, 0:8] = jnp.zeros((3, 8, 128), F32)
        XP[c, :, :, 8:16] = zero_rows[:, 0:3]
        return carry

    lax.fori_loop(0, COLS, clear, 0)
    count = count + halo.greet(barrier)
    for load in loads[5:]:
        load.start()
    for load in loads[0:5]:
        load.wait()
    own_fields(refs)
    pl.semaphore_wait(barrier, count)
    fields, previous = halo.fields(), halo.previous()
    halo.start(fields)
    halo.start(halo.chunk(0))
    halo.start(previous)

    def send(c, carry):
        halo.start(halo.chunk(c))
        return carry

    lax.fori_loop(1, CHUNKS, send, 0)
    for load in loads[5:]:
        load.wait()
    build_operators(refs)
    halo.arrived(fields)
    prepare_fields(refs)

    halo.arrived(halo.chunk(0))
    current_pair(refs, 0)

    def earlier(p, carry):
        previous_pair(refs, p)
        return carry

    def one(p, carry):
        @pl.when(p == PER_CHUNK // 2)
        def _():
            halo.arrived(previous)
            lax.fori_loop(0, PAIRS, earlier, 0)

        @pl.when(p % (PER_CHUNK // 2) == 0)
        def _():
            halo.arrived(halo.chunk(p // (PER_CHUNK // 2)))

        second_pair(refs, p - 1)
        second_pair(refs, PAIRS + p - 1)
        second_pair(refs, 2 * PAIRS + jnp.maximum(p - 2, 0))
        current_pair(refs, p)
        return carry

    lax.fori_loop(1, PAIRS, one, 0)
    for pair in (PAIRS - 1, 2 * PAIRS - 1, 3 * PAIRS - 2, 3 * PAIRS - 1):
        second_pair(refs, pair)
    early, late = Reducer(sizes, refs, "q"), Reducer(sizes, refs, "g")
    stages = len(early.groups)
    early.start(0, refs["QV"][...])

    def sent(c, carry):
        halo.left(halo.chunk(c))
        return carry

    def between():
        early.start(1, early.end(0))

    late.start(0, gram_sums(refs, between))
    halo.left(fields)
    halo.left(previous)
    for i in range(1, stages):
        late.start(i, late.end(i - 1))
        if i == 1:
            lax.fori_loop(0, CHUNKS, sent, 0)
        sums = early.end(i)
        if i + 1 < stages:
            early.start(i + 1, sums)
    refs["sums"][...] = sums
    send_sensitivities(refs, dofs, sums)
    early.sent(range(stages))
    late.sent(range(stages - 1))
    refs["grams"][...] = late.end(stages - 1) / dofs
    end_sensitivities(refs)
    late.sent(range(stages - 1, stages))


def result_kernel(names, *args):
    refs = dict(zip(names, args))
    value = refs["grams"][...]
    quotient_col, _ = quotients(refs["sums"][...])
    packed = jnp.concatenate([value, pltpu.roll(value, 128 - WIDE, 1)], 0)
    lane, row = lane_of(packed), row_of(packed)
    masses = jnp.concatenate(
        [value[:, 2 * WIDE : 2 * WIDE + 1], value[:, 2 * WIDE + 1 : 2 * WIDE + 2]], 0
    )
    turned = jnp.transpose(jnp.concatenate([packed, jnp.zeros((128 - WIDE, 128), F32)], 0))[0:WIDE]
    stiff = jnp.where(row >= lane, packed, turned)
    mass = jnp.where(row == lane, masses, jnp.where(row > lane, turned, packed))
    wide_col = jnp.broadcast_to(quotient_col, (16, 128))
    wide_col = jnp.concatenate([wide_col, wide_col, wide_col], 0)
    on_diagonal = jnp.where((lane == row) & (row < COLS), wide_col, 0.0)
    quotient_row = jnp.broadcast_to(jnp.sum(on_diagonal, axis=0, keepdims=True), (WIDE, 128))
    shifted_row = pltpu.roll(quotient_row, COLS, 1)
    shifted_col = pltpu.roll(wide_col, COLS, 0)
    for name, gram in (("gram_stiff", stiff), ("gram_mass", mass)):
        moved = pltpu.roll(gram, 128 - COLS, 1)
        side = jnp.where(
            lane < COLS, gram, jnp.where(lane < 2 * COLS, gram - shifted_row * moved, moved)
        )
        moved = pltpu.roll(side, WIDE - COLS, 0)
        full = jnp.where(
            row < COLS, side, jnp.where(row < 2 * COLS, side - shifted_col * moved, moved)
        )
        for i in range(3 * COLS):
            refs[name][i] = full[i : i + 1, 0 : 3 * COLS]
    for j in range(COLS):
        quotient = quotient_col[j : j + 1]
        for d in range(3):
            for n in range(2):
                refs["search"][0, j, d, n] = (
                    refs["first"][j, d, n] - quotient * refs["second"][j, d, n]
                )
    real = lax.axis_index("real")
    for n in range(2):
        whole = refs["sens_all"][n]
        refs["sens"][n] = jnp.where(real == 0, whole, pltpu.roll(whole, 64, 1))[:, 0:64]


VMEM_SPEC = pl.BlockSpec(memory_space=pltpu.VMEM)
HBM_SPEC = pl.BlockSpec(memory_space=pltpu.HBM)


def run(kernel, statics, ins, outs, scratch, in_hbm=False, **params):
    names = [*ins, *outs, *scratch]
    result = pl.pallas_call(
        functools.partial(kernel, *statics, names),
        out_shape=[jax.ShapeDtypeStruct(shape, dtype) for shape, dtype in outs.values()],
        in_specs=[HBM_SPEC if in_hbm else VMEM_SPEC for name in ins],
        out_specs=[VMEM_SPEC for _ in outs],
        scratch_shapes=list(scratch.values()),
        compiler_params=pltpu.CompilerParams(**params),
        name=kernel.__name__,
    )(*(pltpu.with_memory_space_constraint(v, pltpu.HBM) if in_hbm else v for v in ins.values()))
    return dict(zip(outs, result))


def step_scratch(sizes):
    out = {name: pltpu.VMEM(shape, dtype) for name, (shape, dtype) in COMPUTE_SCRATCH.items()}
    out["send_sem"] = pltpu.SemaphoreType.DMA((N_HALO,))
    out["recv_sem"] = pltpu.SemaphoreType.DMA((N_HALO,))
    out["local_sem"] = pltpu.SemaphoreType.DMA((12,))
    for i, (_, _, size) in enumerate(reduce_groups(sizes)):
        for tag, rows in (("q", 32), ("g", WIDE // 2)):
            out[f"slots{tag}{i}"] = pltpu.VMEM((size, rows, 128), F32)
            out[f"rsend{tag}{i}"] = pltpu.SemaphoreType.DMA((size,))
            out[f"rrecv{tag}{i}"] = pltpu.SemaphoreType.DMA((size,))
    out["terms"] = pltpu.VMEM((2, 3, 8, 128), F32)
    out["swap_sem"] = pltpu.SemaphoreType.DMA((2,))
    return out


def shards(sizes, current, previous, element_stiffness, preconditioner, modulus, density, solid, clamped):
    size_x, size_y, size_z = modulus.shape
    nx, ny = sizes
    dofs = 3.0 * size_x * size_y * size_z * nx * ny
    ins = dict(
        cur=current[0],
        prev=previous[0],
        precond=preconditioner,
        modulus=modulus,
        density=density,
        solid=solid,
        clamped=clamped,
        elem=element_stiffness,
        **{
            name: jnp.asarray(table, COMPUTE_SCRATCH[name + "_in"][1])
            for name, table in operator_tables().items()
        },
    )
    step = run(
        step_kernel,
        (sizes, dofs),
        ins,
        dict(
            grams=((WIDE // 2, 128), F32),
            sums=((32, 128), F32),
            first=((COLS, 3, 2, 8, 128), F32),
            second=((COLS, 3, 2, 8, 128), F32),
            sens_all=((2, 8, 128), F32),
        ),
        step_scratch(sizes),
        in_hbm=True,
        vmem_limit_bytes=32 * 2**20,
        collective_id=1,
        has_side_effects=True,
    )
    done = run(
        result_kernel,
        (),
        step,
        dict(
            gram_stiff=((3 * COLS, 1, 3 * COLS), F32),
            gram_mass=((3 * COLS, 1, 3 * COLS), F32),
            search=((1, COLS, 3, 2, 8, 128), F32),
            sens=((2, 8, 64), F32),
        ),
        {},
        vmem_limit_bytes=8 * 2**20,
    )
    grams = [jnp.transpose(done[name], (1, 0, 2)) for name in ("gram_stiff", "gram_mass")]
    return *grams, done["search"], done["sens"]


def solution(mesh):
    sizes = (mesh.shape["bx"], mesh.shape["by"])
    return jax.shard_map(
        functools.partial(shards, sizes),
        mesh=mesh,
        in_specs=(
            P("real", None, None, "bx", "by", None),
            P("real", None, None, "bx", "by", None),
            P(),
            P("real", None, "bx", "by", None),
            P("bx", "by", None),
            P("bx", "by", None),
            P("real", "bx", "by", None),
            P("bx", "by"),
        ),
        out_specs=(
            P("real", None, None),
            P("real", None, None),
            P("real", None, None, "bx", "by", None),
            P("bx", "by", "real"),
        ),
        check_vma=False,
    )
```

```python
import functools

import jax
import jax.numpy as jnp
import numpy as np
from jax import lax
from jax.experimental import pallas as pl
from jax.experimental.pallas import tpu as pltpu
from jax.sharding import PartitionSpec as P

MESH = pl.DeviceIdType.MESH
F32 = jnp.float32
BF16 = jnp.bfloat16
COLS = 12
WIDE = 4 * COLS
PAIRS = COLS // 2
CHUNKS = 3
PER_CHUNK = COLS // CHUNKS
NOWHERE = 1000.0
DIRS = [
    (1, 0, (0, 2), (0, 8), 3, 0),
    (-1, 0, (1, 1), (0, 8), 0, 0),
    (1, 1, (0, 2), (0, 2), 3, 8),
    (1, -1, (0, 2), (7, 1), 3, 10),
    (-1, 1, (1, 1), (0, 2), 0, 8),
    (-1, -1, (1, 1), (7, 1), 0, 10),
    (0, 1, (0, 2), (0, 2), 1, 8),
    (0, -1, (0, 2), (7, 1), 1, 10),
]
PREV_DIRS = [
    (1, 0, (0, 1), (0, 8), 2, 0),
    (1, 1, (0, 1), (0, 1), 2, 8),
    (0, 1, (0, 2), (0, 1), 0, 8),
]
N_DIRS = len(DIRS)
N_HALO = N_DIRS * (1 + CHUNKS) + len(PREV_DIRS)


def operator_tables():
    out = []
    for bits in ((0, 1), (1,)):
        half = 96 + 16 * len(bits)
        pick_row = np.zeros((2 * half, 25), np.float32)
        pick_row[:, 24] = -NOWHERE
        for a in range(2):
            for b in range(2):
                for q in range(2):
                    for d in range(3):
                        i = 3 * (4 * a + 2 * b + q) + d
                        for y in range(8):
                            m = a * half + ((b * 2 + q) * 3 + d) * 8 + y
                            pick_row[m, i], pick_row[m, 24] = 1, y - b
                        if b in bits:
                            m = a * half + 96 + (bits.index(b) * 2 + q) * 8 + d
                            pick_row[m, i], pick_row[m, 24] = 1, 8 - b
        out.append(pick_row)
    first, second = [], []
    for a in range(2):
        for d in range(3):
            for q in range(2):
                for row in range(16):
                    first.append((a, d, q, -1 if row == 10 else row if row < 10 else None))
        for planes in ([(0, 0), (1, 0)], [(0, 1), (1, 1)], [(2, 0), (2, 1)]):
            for d, q in planes:
                second += [(a, d, q, y) for y in range(8)]
        for q in range(2):
            second += [(a, d % 3, q, 8 if d < 3 else None) for d in range(8)]
    for rows in (first, second):
        size = 3 * len(rows)
        pick_col = np.zeros((48, 2 * size), np.float32)
        row_y = np.full((8, size), NOWHERE * 2, np.float32)
        for part in range(3):
            for k, (a, d, q, y) in enumerate(rows):
                if y is None:
                    continue
                at = part * len(rows) + k
                row_y[:, at] = y
                for b in range(2):
                    i = 24 * (part == 2) + 3 * (4 * a + 2 * b + q) + d
                    pick_col[i, b * size + at] = 1
        out += [pick_col, row_y]
    row1, row2, col1, y1, col2, y2 = out
    rows = np.concatenate([row1, row2])
    return dict(
        rows=rows[:, 0:24],
        row_ys=np.tile(rows[:, 24:25], (1, 128)),
        cols=np.concatenate([col1, col2], 1),
        col_ys=np.concatenate([y1, y2], 1),
    )


def pick_dot(left, right):
    return lax.dot_general(left, right, (((1,), (0,)), ((), ())), preferred_element_type=F32)


def halves(value):
    high = value.astype(BF16)
    return high, (value - high.astype(F32)).astype(BF16)


def lane_of(value):
    return lax.broadcasted_iota(jnp.int32, value.shape, 1)


def row_of(value):
    return lax.broadcasted_iota(jnp.int32, value.shape, 0)


def from_next_z(value):
    return jnp.where(lane_of(value) == 127, 0.0, pltpu.roll(value, 127, 1))


def to_next_z(value):
    return jnp.where(lane_of(value) == 0, 0.0, pltpu.roll(value, 1, 1))


def spread(row):
    return jnp.broadcast_to(row, (8, 128))


def from_lower_y(main, below):
    return jnp.where(row_of(main) == 0, spread(below), pltpu.roll(main, 1, 0))


def from_upper_y(main, above):
    return jnp.where(row_of(main) == 7, spread(above), pltpu.roll(main, 7, 0))


def stacked_rows(rows):
    out = jnp.zeros((8, 128), F32)
    at = row_of(out)
    for d, row in enumerate(rows):
        out = jnp.where(at == d, spread(row), out)
    return out


def column_rows(index):
    return pl.ds(index, 8, stride=WIDE)


class Halo:
    def __init__(self, sizes, refs):
        self.refs = refs
        self.bx, self.by = lax.axis_index("bx"), lax.axis_index("by")
        self.nx, self.ny = sizes

    def inside(self, dx, dy):
        x, y = self.bx + dx, self.by + dy
        return (x >= 0) & (x < self.nx) & (y >= 0) & (y < self.ny)

    def copy(self, source, target, job, at):
        dx, dy, (x0, xn), (y0, yn), tx, ty = job
        return pltpu.make_async_remote_copy(
            src_ref=source.at[:, :, x0 : x0 + xn, y0 : y0 + yn, :],
            dst_ref=target.at[:, :, tx : tx + xn, ty : ty + yn, :],
            send_sem=self.refs["send_sem"].at[at],
            recv_sem=self.refs["recv_sem"].at[at],
            device_id={"bx": self.bx - dx, "by": self.by - dy},
            device_id_type=MESH,
        )

    def fields(self):
        FE = self.refs["FE"]
        own = FE.at[:, :, 1:3, 0:8, :]
        return [(job, self.copy(own, FE, job, k)) for k, job in enumerate(DIRS)]

    def chunk(self, c):
        part = pl.ds(c * PER_CHUNK, PER_CHUNK)
        source, target = self.refs["cur"].at[part], self.refs["XC"].at[part]
        return [
            (job, self.copy(source, target, job, (c + 1) * N_DIRS + k))
            for k, job in enumerate(DIRS)
        ]

    def previous(self):
        first = N_DIRS * (1 + CHUNKS)
        return [
            (job, self.copy(self.refs["prev"], self.refs["XP"], job, first + k))
            for k, job in enumerate(PREV_DIRS)
        ]

    def start(self, copies):
        for job, copy in copies:
            pl.when(self.inside(-job[0], -job[1]))(copy.start)

    def arrived(self, copies):
        for job, copy in copies:
            pl.when(self.inside(job[0], job[1]))(copy.wait_recv)

    def left(self, copies):
        for job, copy in copies:
            pl.when(self.inside(-job[0], -job[1]))(copy.wait_send)

    def greet(self, barrier):
        count = 0
        for dx in (-1, 0, 1):
            for dy in (-1, 0, 1):
                if dx == 0 and dy == 0:
                    continue
                there = self.inside(dx, dy)

                @pl.when(there)
                def _():
                    pl.semaphore_signal(
                        barrier,
                        inc=1,
                        device_id={"bx": self.bx + dx, "by": self.by + dy},
                        device_id_type=MESH,
                    )

                count = count + there.astype(jnp.int32)
        return count


def own_fields(refs):
    FE = refs["FE"]
    shape = (8, 128)
    lane = lax.broadcasted_iota(jnp.int32, shape, 1)
    row = lax.broadcasted_iota(jnp.int32, shape, 0)
    for x in range(2):
        share = refs["solid_in"][x].astype(F32)
        FE[0, 0, x + 1, 0:8] = refs["modulus_in"][x] * (0.02 + 0.98 * share)
        FE[0, 1, x + 1, 0:8] = refs["density_in"][x] * (0.1 + 0.9 * share)
        held = jnp.broadcast_to(refs["clamped_in"][x : x + 1].astype(F32), (8, 8))
        held = jnp.where(
            lax.broadcasted_iota(jnp.int32, (8, 8), 0) == lax.broadcasted_iota(jnp.int32, (8, 8), 1),
            held,
            0.0,
        )
        held = jnp.sum(held, axis=1, keepdims=True)
        FE[0, 2, x + 1, 0:8] = 1.0 - jnp.where(lane == 0, held, 0.0)


def build_operators(refs):
    high, low = halves(refs["elem_in"][...])
    spread_high = pick_dot(refs["rows_in"][...], high).astype(BF16)
    spread_low = pick_dot(refs["rows_in"][...], low).astype(BF16)
    for row, rows, at, out in ((0, 256, 0, "W1"), (256, 224, 576, "W2")):
        size = refs[out].shape[1]
        cols = refs["cols_in"]
        gap = refs["col_ys_in"][0:1, at : at + size]
        total = 0.0
        for b in range(2):
            columns = slice(2 * at + b * size, 2 * at + (b + 1) * size)
            picked = pick_dot(spread_high[row : row + rows], cols[0:24, columns]) + pick_dot(
                spread_low[row : row + rows], cols[24:48, columns]
            )
            match = gap - refs["row_ys_in"][row : row + rows, 0:1] == float(b)
            total = total + jnp.where(match, picked, 0.0)
        refs[out][...] = total.astype(BF16)


def prepare_fields(refs):
    FE, SS, LM, PM, P8 = refs["FE"], refs["SS"], refs["LM"], refs["PM"], refs["P8"]
    mass_sum = []
    for e in range(4):
        for kind in range(2):
            main, row8 = FE[0, kind, e, 0:8], FE[0, kind, e, 8:9]
            below = FE[0, kind, e, 10:11]
            lower = from_lower_y(main, below)
            here8, lower8 = spread(row8), spread(main[7:8])
            if kind == 0:
                SS[e, 0], SS[e, 1], SS[e, 2], SS[e, 3] = main, lower, here8, lower8
                SS[e, 4] = jnp.where(row_of(lower) == 0, 0.0, lower)
            else:
                mass_sum.append((main + lower, here8 + lower8))
    for n in range(3):
        for part in range(2):
            total = mass_sum[n][part] + mass_sum[n + 1][part]
            keep = FE[0, 2, n + 1, 0:8] if part == 0 else spread(FE[0, 2, n + 1, 8:9])
            LM[n, part] = (total + to_next_z(total)) * 0.125 * keep
        for d in range(3):
            PM[n, d] = FE[1, d, n + 1, 0:8] * FE[0, 2, n + 1, 0:8]
        P8[n] = stacked_rows([FE[1, d, n + 1, 8:9] * FE[0, 2, n + 1, 8:9] for d in range(3)])


def forces(weights, high, low):
    stacked = jnp.concatenate([high, low, high], 0)
    return lax.dot_general(
        weights, stacked, (((1,), (0,)), ((), ())), preferred_element_type=F32
    )


def block_of(force, row, h):
    return force[row : row + 8, h * 128 : h * 128 + 128]


def add_to(store, key, value):
    store[key] = value if key not in store else store[key] + value


def store_halves(high_ref, low_ref, lead, row, h, value):
    high, low = halves(value)
    at = (*lead, slice(row, row + 16), slice(h * 128, h * 128 + 128))
    high_ref[at] = high
    low_ref[at] = low


def store_second(refs, kind, lead, h, planes, edge):
    moved = [from_next_z(plane) for plane in planes]
    blocks = [
        (planes[0], planes[1]),
        (moved[0], moved[1]),
        (planes[2], moved[2]),
        (edge, from_next_z(edge)),
    ]
    for k, block in enumerate(blocks):
        store_halves(
            refs[f"U2H{kind}"], refs[f"U2L{kind}"], lead, k * 16, h, jnp.concatenate(block, 0)
        )


def current_pair(refs, p):
    XC, FE, VV, UH, UL = refs["XC"], refs["FE"], refs["VV"], refs["UH"], refs["UL"]
    SS, LM, PM, P8 = refs["SS"], refs["LM"], refs["PM"], refs["P8"]
    XS, KS, X8, K8 = refs["XS"], refs["KS"], refs["X8"], refs["K8"]
    edge = {}
    for h in range(2):
        for x in range(5):
            keep = FE[0, 2, x]
            rows = []
            for d in range(3):
                value = XC[2 * p + h, d, x] * keep
                moved = from_next_z(value)
                store_halves(UH, UL, (x,), (d * 2) * 16, h, value)
                store_halves(UH, UL, (x,), (d * 2 + 1) * 16, h, moved)
                if 1 <= x <= 3:
                    VV[h, d, 0, x - 1] = value
                    VV[h, d, 1, x - 1] = moved
                rows.append(value[8:9])
            if 1 <= x <= 3:
                edge[h, 0, x] = stacked_rows(rows)
                edge[h, 1, x] = from_next_z(edge[h, 0, x])
    total, total8, energy, energy8 = {}, {}, {}, {}
    for e in range(4):
        high = UH[e : e + 2].reshape(192, 256)
        low = UL[e : e + 2].reshape(192, 256)
        used = [a for a in range(2) if 0 <= e - 1 + a <= 2]
        force = forces(refs["W1"][used[0] * 128 : used[-1] * 128 + 128, :], high, low)
        for a in used:
            n = e - 1 + a
            start = (a - used[0]) * 128
            for h in range(2):
                for b in range(2):
                    for q in range(2):
                        for d in range(3):
                            block = block_of(force, start + ((b * 2 + q) * 3 + d) * 8, h)
                            add_to(total, (n, d, q, h), SS[e, b] * block)
                            if e in (1, 2):
                                add_to(energy, (e, b, h), VV[h, d, q, e + a - 1, 0:8] * block)
                        block = block_of(force, start + 96 + (b * 2 + q) * 8, h)
                        add_to(total8, (n, q, h), SS[e, 2 + b] * block)
                        if e in (1, 2) and b == 1:
                            add_to(energy8, (e, h), edge[h, q, e + a] * block)
    zero = jnp.zeros((8, 128), F32)
    for h in range(2):
        c = 2 * p + h
        for n in range(3):
            stiff8 = total8[n, 0, h] + to_next_z(total8[n, 1, h])
            first8 = P8[n] * stiff8
            second8 = P8[n] * LM[n, 1] * edge[h, 0, n + 1]
            for ref, col, value in (
                (X8, 0, edge[h, 0, n + 1]),
                (X8, 1, first8),
                (X8, 2, second8),
                (K8, 0, zero),
            ):
                ref[n, column_rows(col * COLS + c), :] = value
            firsts, seconds = [], []
            for d in range(3):
                stiff = total[n, d, 0, h] + to_next_z(total[n, d, 1, h])
                here = VV[h, d, 0, n, 0:8]
                firsts.append(PM[n, d] * stiff)
                seconds.append(PM[n, d] * LM[n, 0] * here)
                for ref, col, value in (
                    (XS, 0, here),
                    (XS, 1, firsts[d]),
                    (XS, 2, seconds[d]),
                    (KS, 0, stiff if n < 2 else zero),
                ):
                    ref[d * 3 + n, column_rows(col * COLS + c), :] = value
                if n < 2:
                    refs["first"][c, d, n] = firsts[d]
                    refs["second"][c, d, n] = seconds[d]
            store_second(refs, 0, (p, n), h, firsts, first8)
            store_second(refs, 1, (p, n), h, seconds, second8)
        top, bottom = 0.0, 0.0
        for n in range(2):
            for d in range(3):
                here = VV[h, d, 0, n, 0:8]
                stiff = total[n, d, 0, h] + to_next_z(total[n, d, 1, h])
                top = top + here * stiff
                bottom = bottom + here * here * LM[n, 0]
        refs["QV"][pl.ds(c, 1), :] = jnp.sum(top, axis=0, keepdims=True)
        refs["QV"][pl.ds(16 + c, 1), :] = jnp.sum(bottom, axis=0, keepdims=True)
        for e in (1, 2):
            above = jnp.sum(energy8[e, h], axis=0, keepdims=True)
            refs["ES"][c, e - 1] = energy[e, 0, h] + from_upper_y(energy[e, 1, h], above)
            square = 0.0
            for x in (e - 1, e):
                for d in range(3):
                    for q in range(2):
                        square = square + VV[h, d, q, x] * VV[h, d, q, x]
            main = square[0:8]
            refs["EM"][c, e - 1] = (main + from_upper_y(main, square[8:9])) * 0.125


def previous_pair(refs, p):
    for h in range(2):
        c = 2 * p + h
        at = column_rows(3 * COLS + c)
        for n in range(3):
            rows, planes = [], []
            for d in range(3):
                value = refs["XP"][c, d, n] * refs["FE"][0, 2, n + 1]
                planes.append(value[0:8])
                refs["XS"][d * 3 + n, at, :] = planes[d]
                rows.append(value[8:9])
            edge = stacked_rows(rows)
            refs["X8"][n, at, :] = edge
            store_second(refs, 2, (p, n), h, planes, edge)


def second_pair(refs, kind, p):
    SS, KS, K8 = refs["SS"], refs["KS"], refs["K8"]
    total, total8 = {}, {}
    for e in range(2):
        high = refs[f"U2H{kind}"][p, e : e + 2].reshape(128, 256)
        low = refs[f"U2L{kind}"][p, e : e + 2].reshape(128, 256)
        force = forces(refs["W2"][...], high, low)
        for a in range(2):
            n = e + a
            for h in range(2):
                for q in range(2):
                    for b in range(2):
                        for d in range(3):
                            block = block_of(force, a * 112 + ((b * 2 + q) * 3 + d) * 8, h)
                            add_to(total, (n, d, q, h), SS[e + 1, 4 * b] * block)
                    add_to(
                        total8, (n, q, h), SS[e + 1, 3] * block_of(force, a * 112 + 96 + q * 8, h)
                    )
    for h in range(2):
        at = column_rows((kind + 1) * COLS + 2 * p + h)
        for n in range(3):
            K8[n, at, :] = total8[n, 0, h] + to_next_z(total8[n, 1, h])
            for d in range(3):
                KS[d * 3 + n, at, :] = total[n, d, 0, h] + to_next_z(total[n, d, 1, h])


def put_halves(ref, row, rows_low, lanes, value):
    high, low = halves(value)
    ref[row : row + WIDE, lanes] = high
    ref[rows_low + row : rows_low + row + WIDE, lanes] = low


def gram_sums(refs, between):
    XS, KS, X8, K8, LM = refs["XS"], refs["KS"], refs["X8"], refs["K8"], refs["LM"]
    GX, GY, FT = refs["GX"], refs["GY"], refs["FT"]

    def product(slot, width):
        return lax.dot_general(
            GX[slot, :, 0:width],
            GY[slot, :, 0:width],
            (((1,), (1,)), ((), ())),
            preferred_element_type=F32,
        )

    total = jnp.zeros((2 * WIDE, 4 * WIDE), F32)
    for i in range(6):
        d, n = i // 2, i % 2
        for y in range(8):
            lanes = slice(y * 128, y * 128 + 128)
            rows = slice(y * WIDE, (y + 1) * WIDE)
            value = XS[d * 3 + n, rows, :]
            put_halves(GX.at[i % 2], 0, WIDE, lanes, value)
            put_halves(GY.at[i % 2], 0, 2 * WIDE, lanes, KS[d * 3 + n, rows, :])
            put_halves(GY.at[i % 2], WIDE, 2 * WIDE, lanes, value * LM[n, 0, y : y + 1])
        total = total + product(i % 2, 1024)
        if i == 3:
            between()
    for slot in range(2):
        GY[slot] = jnp.zeros(GY.shape[1:], BF16)
    for d in range(3):
        for y in range(8):
            lanes = slice(y * 128, y * 128 + 128)
            rows = slice(y * WIDE, (y + 1) * WIDE)
            put_halves(GX.at[d % 2], 0, WIDE, lanes, XS[d * 3 + 2, rows, :])
            put_halves(GY.at[d % 2], 0, 2 * WIDE, lanes, KS[d * 3 + 2, rows, :])
        total = total + product(d % 2, 1024)
    for n in range(3):
        for d in range(3):
            lanes = slice((n * 3 + d) * 128, (n * 3 + d) * 128 + 128)
            rows = slice(d * WIDE, (d + 1) * WIDE)
            put_halves(GX.at[1], 0, WIDE, lanes, X8[n, rows, :])
            put_halves(GY.at[1], 0, 2 * WIDE, lanes, K8[n, rows, :])
    total = total + product(1, 1152)
    FT[...] = jnp.zeros(FT.shape, F32)
    FT[:, 0 : 4 * WIDE] = total[0:WIDE] + total[WIDE : 2 * WIDE]
    wide = FT[...]
    stiff = wide[:, 0:128] + pltpu.roll(wide, 256 - 2 * WIDE, 1)[:, 0:128]
    mass = pltpu.roll(stiff, 128 - WIDE, 1)
    lane, row = lane_of(stiff), row_of(stiff)
    packed = jnp.where(row >= lane, stiff, mass)
    diagonal = jnp.sum(jnp.where(row == lane, mass, 0.0), axis=1, keepdims=True)
    half = WIDE // 2
    lane = lane[0:half]
    out = jnp.where(lane < WIDE, packed[0:half], pltpu.roll(packed[half:WIDE], WIDE, 1))
    out = jnp.where(lane < 2 * WIDE, out, 0.0)
    out = jnp.where(lane == 2 * WIDE, diagonal[0:half], out)
    return jnp.where(lane == 2 * WIDE + 1, diagonal[half:WIDE], out)


COMPUTE_SCRATCH = {
    "XC": ((COLS, 3, 5, 16, 128), F32),
    "XP": ((COLS, 3, 3, 16, 128), F32),
    "FE": ((2, 3, 5, 16, 128), F32),
    "modulus_in": ((2, 8, 128), F32),
    "density_in": ((2, 8, 128), F32),
    "solid_in": ((2, 8, 128), jnp.int32),
    "clamped_in": ((2, 8), jnp.int32),
    "elem_in": ((24, 24), F32),
    "rows_in": ((480, 24), BF16),
    "row_ys_in": ((480, 128), F32),
    "cols_in": ((48, 1920), BF16),
    "col_ys_in": ((8, 960), F32),
    "W1": ((256, 576), BF16),
    "W2": ((224, 384), BF16),
    "SS": ((4, 5, 8, 128), F32),
    "LM": ((3, 2, 8, 128), F32),
    "PM": ((3, 3, 8, 128), F32),
    "P8": ((3, 8, 128), F32),
    "VV": ((2, 3, 2, 3, 16, 128), F32),
    "UH": ((5, 96, 256), BF16),
    "UL": ((5, 96, 256), BF16),
    **{f"U2{part}{kind}": ((PAIRS, 3, 64, 256), BF16) for part in "HL" for kind in range(3)},
    "XS": ((9, WIDE * 8, 128), F32),
    "KS": ((9, WIDE * 8, 128), F32),
    "X8": ((3, WIDE * 8, 128), F32),
    "K8": ((3, WIDE * 8, 128), F32),
    "GX": ((2, 2 * WIDE, 1152), BF16),
    "GY": ((2, 4 * WIDE, 1152), BF16),
    "FT": ((WIDE, 256), F32),
    "QV": ((32, 128), F32),
    "ES": ((COLS, 2, 8, 128), F32),
    "EM": ((COLS, 2, 8, 128), F32),
}


def reduce_groups(sizes):
    nx, ny = sizes
    groups = [("bx", 1, 2), ("bx", 2, nx // 2), ("by", 1, ny)]
    return [g for g in groups if g[2] > 1]


def peers_of(axis, stride, size):
    at = lax.axis_index(axis)
    place = (at // stride) % size
    base = at - place * stride
    peers = [lax.rem(place + k, size) for k in range(1, size)]
    return place, [(there, base + there * stride) for there in peers]


def greet_reducers(sizes, barrier):
    count = 0
    for axis, stride, size in reduce_groups(sizes):
        for _, peer in peers_of(axis, stride, size)[1]:
            pl.semaphore_signal(barrier, inc=1, device_id={axis: peer}, device_id_type=MESH)
            count += 1
    pl.semaphore_signal(
        barrier, inc=1, device_id={"real": 1 - lax.axis_index("real")}, device_id_type=MESH
    )
    return count + 1


class Reducer:
    def __init__(self, sizes, refs, tag):
        self.refs, self.tag, self.groups = refs, tag, reduce_groups(sizes)

    def part(self, name, i):
        return self.refs[f"{name}{self.tag}{i}"]

    def copy(self, i, place, slot, peer, k):
        return pltpu.make_async_remote_copy(
            src_ref=self.part("slots", i).at[place],
            dst_ref=self.part("slots", i).at[slot],
            send_sem=self.part("rsend", i).at[k],
            recv_sem=self.part("rrecv", i).at[slot],
            device_id={self.groups[i][0]: peer},
            device_id_type=MESH,
        )

    def start(self, i, value):
        place, peers = peers_of(*self.groups[i])
        self.part("slots", i)[place] = value
        for k, (_, peer) in enumerate(peers):
            self.copy(i, place, place, peer, k).start()

    def end(self, i):
        place, peers = peers_of(*self.groups[i])
        for k, (there, peer) in enumerate(peers):
            self.copy(i, place, there, peer, k).wait_recv()
        slots = self.part("slots", i)
        value = slots[0]
        for k in range(1, self.groups[i][2]):
            value = value + slots[k]
        return value

    def sent(self, stages):
        for i in stages:
            place, peers = peers_of(*self.groups[i])
            for k, (_, peer) in enumerate(peers):
                self.copy(i, place, place, peer, k).wait_send()


def quotients(sums):
    sums = jnp.sum(sums, axis=1, keepdims=True)
    return sums[0:16] / sums[16:32], sums[16:32]


def send_sensitivities(refs, dofs, sums):
    quotient_col, denominator_col = quotients(sums)
    denominator_col = denominator_col / dofs
    weights, power_sum = [], jnp.zeros((1, 1), F32)
    for j in range(COLS):
        quotient = quotient_col[j : j + 1]
        inverse = 1.0 / quotient
        square = inverse * inverse
        powered = square * square
        power_sum = power_sum + powered
        weights.append((quotient, powered / denominator_col[j : j + 1]))
    terms = refs["terms"]
    for n in range(2):
        stiff_sum = jnp.zeros((8, 128), F32)
        mass_sum = jnp.zeros((8, 128), F32)
        for j, (quotient, weight) in enumerate(weights):
            stiff_sum = stiff_sum + weight * refs["ES"][j, n]
            mass_sum = mass_sum + (weight * quotient) * refs["EM"][j, n]
        terms[0, n] = (
            3.0 * refs["FE"][0, 0, n + 1, 0:8] * stiff_sum
            - refs["FE"][0, 1, n + 1, 0:8] * mass_sum
        )
    terms[0, 2] = jnp.broadcast_to(power_sum, (8, 128))
    swap_of(refs).start()


def swap_of(refs):
    return pltpu.make_async_remote_copy(
        src_ref=refs["terms"].at[0],
        dst_ref=refs["terms"].at[1],
        send_sem=refs["swap_sem"].at[0],
        recv_sem=refs["swap_sem"].at[1],
        device_id={"real": 1 - lax.axis_index("real")},
        device_id_type=MESH,
    )


def end_sensitivities(refs):
    swap_of(refs).wait()
    terms = refs["terms"]
    overall = terms[0, 2] + terms[1, 2]
    for n in range(2):
        refs["sens_all"][n] = (terms[0, n] + terms[1, n]) / overall


def step_kernel(sizes, dofs, names, *args):
    refs = dict(zip(names, args))
    halo = Halo(sizes, refs)
    barrier = pltpu.get_barrier_semaphore()
    FE, XC, XP, local_sem = refs["FE"], refs["XC"], refs["XP"], refs["local_sem"]
    pairs = [
        (refs["modulus"], refs["modulus_in"]),
        (refs["density"], refs["density_in"]),
        (refs["solid"].at[0], refs["solid_in"]),
        (refs["clamped"], refs["clamped_in"]),
        (refs["precond"], FE.at[1:2, :, 1:3, 0:8, :]),
        (refs["cur"], XC.at[:, :, 1:3, 0:8, :]),
        (refs["prev"], XP.at[:, :, 0:2, 0:8, :]),
        *((refs[name], refs[name + "_in"]) for name in ("elem", "rows", "row_ys", "cols", "col_ys")),
    ]
    loads = [pltpu.make_async_copy(a, b, local_sem.at[k]) for k, (a, b) in enumerate(pairs)]
    for load in loads[0:4]:
        load.start()
    count = greet_reducers(sizes, barrier)
    refs["QV"][...] = jnp.zeros((32, 128), F32)
    for k in range(2):
        FE[k] = jnp.zeros(FE.shape[1:], F32)
    loads[4].start()
    zero_rows = jnp.zeros((3, 5, 8, 128), F32)

    def clear(c, carry):
        for x in (0, 3, 4):
            XC[c, :, x, 0:8] = jnp.zeros((3, 8, 128), F32)
        XC[c, :, :, 8:16] = zero_rows
        XP[c, :, 2, 0:8] = jnp.zeros((3, 8, 128), F32)
        XP[c, :, :, 8:16] = zero_rows[:, 0:3]
        return carry

    lax.fori_loop(0, COLS, clear, 0)
    count = count + halo.greet(barrier)
    for load in loads[5:]:
        load.start()
    for load in loads[0:5]:
        load.wait()
    own_fields(refs)
    pl.semaphore_wait(barrier, count)
    fields, previous = halo.fields(), halo.previous()
    halo.start(fields)
    halo.start(halo.chunk(0))
    halo.start(previous)

    def send(c, carry):
        halo.start(halo.chunk(c))
        return carry

    lax.fori_loop(1, CHUNKS, send, 0)
    for load in loads[5:]:
        load.wait()
    build_operators(refs)
    halo.arrived(fields)
    prepare_fields(refs)

    halo.arrived(halo.chunk(0))
    current_pair(refs, 0)

    def earlier(p, carry):
        previous_pair(refs, p)
        return carry

    def one(p, carry):
        @pl.when(p == PER_CHUNK // 2)
        def _():
            halo.arrived(previous)
            lax.fori_loop(0, PAIRS, earlier, 0)

        @pl.when(p % (PER_CHUNK // 2) == 0)
        def _():
            halo.arrived(halo.chunk(p // (PER_CHUNK // 2)))

        second_pair(refs, 0, p - 1)
        second_pair(refs, 1, p - 1)
        current_pair(refs, p)
        second_pair(refs, 2, jnp.maximum(p - 2, 0))
        return carry

    lax.fori_loop(1, PAIRS, one, 0)
    for kind, pair in ((0, PAIRS - 1), (1, PAIRS - 1), (2, PAIRS - 2), (2, PAIRS - 1)):
        second_pair(refs, kind, pair)
    early, late = Reducer(sizes, refs, "q"), Reducer(sizes, refs, "g")
    stages = len(early.groups)
    early.start(0, refs["QV"][...])

    def sent(c, carry):
        halo.left(halo.chunk(c))
        return carry

    def between():
        early.start(1, early.end(0))

    late.start(0, gram_sums(refs, between))
    halo.left(fields)
    halo.left(previous)
    for i in range(1, stages):
        late.start(i, late.end(i - 1))
        if i == 1:
            lax.fori_loop(0, CHUNKS, sent, 0)
        sums = early.end(i)
        if i + 1 < stages:
            early.start(i + 1, sums)
    refs["sums"][...] = sums
    send_sensitivities(refs, dofs, sums)
    early.sent(range(stages))
    late.sent(range(stages - 1))
    refs["grams"][...] = late.end(stages - 1) / dofs
    end_sensitivities(refs)
    late.sent(range(stages - 1, stages))


def result_kernel(names, *args):
    refs = dict(zip(names, args))
    value = refs["grams"][...]
    quotient_col, _ = quotients(refs["sums"][...])
    packed = jnp.concatenate([value, pltpu.roll(value, 128 - WIDE, 1)], 0)
    lane, row = lane_of(packed), row_of(packed)
    masses = jnp.concatenate(
        [value[:, 2 * WIDE : 2 * WIDE + 1], value[:, 2 * WIDE + 1 : 2 * WIDE + 2]], 0
    )
    turned = jnp.transpose(jnp.concatenate([packed, jnp.zeros((128 - WIDE, 128), F32)], 0))[0:WIDE]
    stiff = jnp.where(row >= lane, packed, turned)
    mass = jnp.where(row == lane, masses, jnp.where(row > lane, turned, packed))
    wide_col = jnp.broadcast_to(quotient_col, (16, 128))
    wide_col = jnp.concatenate([wide_col, wide_col, wide_col], 0)
    on_diagonal = jnp.where((lane == row) & (row < COLS), wide_col, 0.0)
    quotient_row = jnp.broadcast_to(jnp.sum(on_diagonal, axis=0, keepdims=True), (WIDE, 128))
    shifted_row = pltpu.roll(quotient_row, COLS, 1)
    shifted_col = pltpu.roll(wide_col, COLS, 0)
    for name, gram in (("gram_stiff", stiff), ("gram_mass", mass)):
        moved = pltpu.roll(gram, 128 - COLS, 1)
        side = jnp.where(
            lane < COLS, gram, jnp.where(lane < 2 * COLS, gram - shifted_row * moved, moved)
        )
        moved = pltpu.roll(side, WIDE - COLS, 0)
        full = jnp.where(
            row < COLS, side, jnp.where(row < 2 * COLS, side - shifted_col * moved, moved)
        )
        for i in range(3 * COLS):
            refs[name][i] = full[i : i + 1, 0 : 3 * COLS]
    for j in range(COLS):
        quotient = quotient_col[j : j + 1]
        for d in range(3):
            for n in range(2):
                refs["search"][0, j, d, n] = (
                    refs["first"][j, d, n] - quotient * refs["second"][j, d, n]
                )
    real = lax.axis_index("real")
    for n in range(2):
        whole = refs["sens_all"][n]
        refs["sens"][n] = jnp.where(real == 0, whole, pltpu.roll(whole, 64, 1))[:, 0:64]


VMEM_SPEC = pl.BlockSpec(memory_space=pltpu.VMEM)
HBM_SPEC = pl.BlockSpec(memory_space=pltpu.HBM)


def run(kernel, statics, ins, outs, scratch, in_hbm=False, **params):
    names = [*ins, *outs, *scratch]
    result = pl.pallas_call(
        functools.partial(kernel, *statics, names),
        out_shape=[jax.ShapeDtypeStruct(shape, dtype) for shape, dtype in outs.values()],
        in_specs=[HBM_SPEC if in_hbm else VMEM_SPEC for name in ins],
        out_specs=[VMEM_SPEC for _ in outs],
        scratch_shapes=list(scratch.values()),
        compiler_params=pltpu.CompilerParams(**params),
        name=kernel.__name__,
    )(*(pltpu.with_memory_space_constraint(v, pltpu.HBM) if in_hbm else v for v in ins.values()))
    return dict(zip(outs, result))


def step_scratch(sizes):
    out = {name: pltpu.VMEM(shape, dtype) for name, (shape, dtype) in COMPUTE_SCRATCH.items()}
    out["send_sem"] = pltpu.SemaphoreType.DMA((N_HALO,))
    out["recv_sem"] = pltpu.SemaphoreType.DMA((N_HALO,))
    out["local_sem"] = pltpu.SemaphoreType.DMA((12,))
    for i, (_, _, size) in enumerate(reduce_groups(sizes)):
        for tag, rows in (("q", 32), ("g", WIDE // 2)):
            out[f"slots{tag}{i}"] = pltpu.VMEM((size, rows, 128), F32)
            out[f"rsend{tag}{i}"] = pltpu.SemaphoreType.DMA((size,))
            out[f"rrecv{tag}{i}"] = pltpu.SemaphoreType.DMA((size,))
    out["terms"] = pltpu.VMEM((2, 3, 8, 128), F32)
    out["swap_sem"] = pltpu.SemaphoreType.DMA((2,))
    return out


def shards(sizes, current, previous, element_stiffness, preconditioner, modulus, density, solid, clamped):
    size_x, size_y, size_z = modulus.shape
    nx, ny = sizes
    dofs = 3.0 * size_x * size_y * size_z * nx * ny
    ins = dict(
        cur=current[0],
        prev=previous[0],
        precond=preconditioner,
        modulus=modulus,
        density=density,
        solid=solid,
        clamped=clamped,
        elem=element_stiffness,
        **{
            name: jnp.asarray(table, COMPUTE_SCRATCH[name + "_in"][1])
            for name, table in operator_tables().items()
        },
    )
    step = run(
        step_kernel,
        (sizes, dofs),
        ins,
        dict(
            grams=((WIDE // 2, 128), F32),
            sums=((32, 128), F32),
            first=((COLS, 3, 2, 8, 128), F32),
            second=((COLS, 3, 2, 8, 128), F32),
            sens_all=((2, 8, 128), F32),
        ),
        step_scratch(sizes),
        in_hbm=True,
        vmem_limit_bytes=32 * 2**20,
        collective_id=1,
        has_side_effects=True,
    )
    done = run(
        result_kernel,
        (),
        step,
        dict(
            gram_stiff=((3 * COLS, 1, 3 * COLS), F32),
            gram_mass=((3 * COLS, 1, 3 * COLS), F32),
            search=((1, COLS, 3, 2, 8, 128), F32),
            sens=((2, 8, 64), F32),
        ),
        {},
        vmem_limit_bytes=8 * 2**20,
    )
    grams = [jnp.transpose(done[name], (1, 0, 2)) for name in ("gram_stiff", "gram_mass")]
    return *grams, done["search"], done["sens"]


def solution(mesh):
    sizes = (mesh.shape["bx"], mesh.shape["by"])
    return jax.shard_map(
        functools.partial(shards, sizes),
        mesh=mesh,
        in_specs=(
            P("real", None, None, "bx", "by", None),
            P("real", None, None, "bx", "by", None),
            P(),
            P("real", None, "bx", "by", None),
            P("bx", "by", None),
            P("bx", "by", None),
            P("real", "bx", "by", None),
            P("bx", "by"),
        ),
        out_specs=(
            P("real", None, None),
            P("real", None, None),
            P("real", None, None, "bx", "by", None),
            P("bx", "by", "real"),
        ),
        check_vma=False,
    )
```
